512 devices in a mesh: dp: 16 (over y_hi, x), fsdp: 32 (over z, y_lo, core).
Axes of the slice: x: 4, y: 8 (y_hi: 4, y_lo: 2; y = y_hi * 2 + y_lo), z: 8, core: 2. Of those that a mesh axis runs over, the one named last changes fastest.
Arguments:
- tokens: bfloat16 [65536, 8192], P(('dp', 'fsdp')), may hold values from -6 to 6
- frozen_key_matrix: bfloat16 [8192, 512], P('fsdp'), may hold values from -0.0625 to 0.0625
- adapter_down_factor: float32 [96, 8192, 16], P('fsdp', 'dp'), may hold values from -0.0625 to 0.0625
- adapter_up_factor: float32 [96, 16, 512], P('fsdp', None, 'dp'), may hold values from -1.5 to 1.5
- key_norm_gain: float32 [128], replicated, may hold values from 0.1 to 1.9
- adapter_offset: int32 [16, 32], P('dp', 'fsdp'), may hold values from 0 to 2, as said below
- loss_row_count: int32 [16, 32], P('dp', 'fsdp'), may hold values from 32 to 128, as said below
- cotangent: bfloat16 [65536, 512], P(('dp', 'fsdp')), may hold values from -6 to 6
Outputs:
- keys: bfloat16 [65536, 512], P(('dp', 'fsdp'))
- input_grad: bfloat16 [65536, 8192], P(('dp', 'fsdp'))
- down_grad: float32 [96, 8192, 16], P('fsdp', 'dp')
- up_factor_gradient: float32 [96, 16, 512], P('fsdp', None, 'dp')
The draws below stay inside these ranges and needn't reach their ends.
Inputs may be any that keep to these rules, and one draw needn't show every extreme that they name: `adapter_offset`: in every column j, each offset 0 to 2 is named by at least one dp index. `loss_row_count`: some block has 128 live rows and some block 32.
All inputs are finite; a program needn't handle non-finite values.
Results may differ from the reference program's by a relative error of at most 0.0033.
Values may be sent and summed in bfloat16 or wider, within the bound.
A program may use at most 64 MiB of HBM per device.

```python
import jax
import jax.numpy as jnp
from jax import lax

MODEL_WIDTH = 8192
HD = 128
ADAPTER_RANK = 16
BLOCK_ROWS = 128
ADP_DEV = 3
KEY_WINDOW_WIDTH = 512
ADAPTER_COUNT = 96
DATA_GROUPS = 16
SHARDS = 32
TOKENS = 65536
N_DP = 16
N_FSDP = 32


def draw_adapter_offset(key, part):
    first_key, second_key = jax.random.split(jax.random.fold_in(key, 11))
    picked = jax.random.randint(first_key, (DATA_GROUPS, SHARDS), 0, ADP_DEV * ADP_DEV)
    skewed = jnp.minimum(picked % ADP_DEV, picked // ADP_DEV)
    positions = jnp.arange(DATA_GROUPS, dtype=jnp.int32)[:, None]
    values = jnp.where(positions < ADP_DEV, jnp.broadcast_to(positions % ADP_DEV, (DATA_GROUPS, SHARDS)), skewed)
    scores = jax.random.randint(second_key, (DATA_GROUPS, SHARDS), 0, 2 ** 20) * DATA_GROUPS + positions
    order = jnp.argsort(scores, axis=0, stable=True)
    return jnp.take_along_axis(values, order, axis=0).astype(jnp.int32)


def draw_loss_row_count(key, part):
    first_key, second_key, third_key = jax.random.split(jax.random.fold_in(key, 23), 3)
    total = DATA_GROUPS * SHARDS
    values = jax.random.randint(first_key, (total,), BLOCK_ROWS // 4, BLOCK_ROWS + 1)
    high_pos = jax.random.randint(second_key, (), 0, total)
    low_pos = (high_pos + 1 + jax.random.randint(third_key, (), 0, total - 1)) % total
    index = jnp.arange(total, dtype=jnp.int32)
    values = jnp.where(index == high_pos, BLOCK_ROWS, values)
    values = jnp.where(index == low_pos, BLOCK_ROWS // 4, values)
    return values.reshape(DATA_GROUPS, SHARDS).astype(jnp.int32)


def steps_of(key, dims, pieces, least, largest):
    level, own = 1.0, jax.random.fold_in(key, 6)
    for position, shards_of in pieces:
        steps = jnp.exp(jax.random.uniform(jax.random.fold_in(own, position), (shards_of,), jnp.float32, least / len(pieces), largest / len(pieces)))
        level = level * jnp.repeat(steps, dims[position] // shards_of).reshape([-1 if axis == position else 1 for axis in range(len(dims))])
    return level


def normal_values(key, shape, spread, bound, pieces=(), held_as=jnp.bfloat16):
    factor_of = steps_of(key, shape, pieces, -0.22, 0.18) if pieces else 1.0
    values = jax.random.normal(key, shape, jnp.float32) * spread * factor_of
    return jnp.minimum(jnp.maximum(values, -bound), bound).astype(held_as)


def setup_inputs(seed: int = 0) -> dict:
    key_of = jax.random.split(jax.random.key(seed), 9)
    return {
        "tokens": normal_values(key_of[0], (TOKENS, MODEL_WIDTH), 1.0, 6.0, ((0, 512),)),
        "frozen_key_matrix": normal_values(key_of[1], (MODEL_WIDTH, KEY_WINDOW_WIDTH), MODEL_WIDTH ** -0.5, 0.0625, ((0, 32),)),
        "adapter_down_factor": normal_values(key_of[2], (ADAPTER_COUNT, MODEL_WIDTH, ADAPTER_RANK), MODEL_WIDTH ** -0.5, 0.0625, ((0, 32), (1, 16)), jnp.float32),
        "adapter_up_factor": normal_values(key_of[3], (ADAPTER_COUNT, ADAPTER_RANK, KEY_WINDOW_WIDTH), ADAPTER_RANK ** -0.5, 1.5, ((0, 32), (2, 16)), jnp.float32),
        "key_norm_gain": jnp.clip(1.0 + 0.18 * jax.random.normal(key_of[4], (HD,), jnp.float32), 0.1, 1.9),
        "adapter_offset": draw_adapter_offset(jax.random.fold_in(key_of[8], 71), 0),
        "loss_row_count": draw_loss_row_count(jax.random.fold_in(key_of[8], 71), 0),
        "cotangent": normal_values(key_of[7], (TOKENS, KEY_WINDOW_WIDTH), 2.0, 6.0, ((0, 512),)),
    }


adapter_scale = 2.0
norm_eps = 1e-06

def block_pass(block_tokens, weight, down_projection, up_projection, key_norm_gain, live_count, adapter_total, block_cot):
    row_count = block_tokens.shape[0]
    highest_precision = lax.Precision.HIGHEST
    tokens_float = block_tokens.astype(jnp.float32)
    frozen_output = jnp.dot(block_tokens, weight, preferred_element_type=jnp.float32)
    lowrank_output = jnp.dot(tokens_float, down_projection, precision=highest_precision)
    projected_keys = frozen_output + adapter_scale * jnp.dot(lowrank_output, up_projection, precision=highest_precision)
    shaped = projected_keys.reshape(row_count, -1, HD)
    mean_square = lax.optimization_barrier(jnp.mean(shaped * shaped, axis=-1, keepdims=True))
    inverse_rms = lax.rsqrt(mean_square + norm_eps)
    normed = shaped * inverse_rms
    keys = (normed * key_norm_gain).reshape(row_count, -1).astype(jnp.bfloat16)
    row_mask = (jnp.arange(row_count, dtype=jnp.int32) < live_count).astype(jnp.float32)
    row_grad = block_cot.astype(jnp.float32) * row_mask[:, None] * (row_count / adapter_total)
    scaled_grad = row_grad.reshape(normed.shape) * key_norm_gain
    along_norm = lax.optimization_barrier(jnp.mean(scaled_grad * normed, axis=-1, keepdims=True))
    prenorm_gradient = (inverse_rms * (scaled_grad - normed * along_norm)).reshape(row_count, -1)
    pre_grad_low = prenorm_gradient.astype(jnp.bfloat16)
    lowrank_gradient = adapter_scale * jnp.dot(prenorm_gradient, up_projection.T, precision=highest_precision)
    input_base = lax.dot_general(pre_grad_low, weight, (((1,), (1,)), ((), ())), preferred_element_type=jnp.float32)
    input_grad = (input_base + jnp.dot(lowrank_gradient, down_projection.T, precision=highest_precision)).astype(jnp.bfloat16)
    down_grad = lax.dot_general(tokens_float, lowrank_gradient, (((0,), (0,)), ((), ())), precision=highest_precision)
    up_factor_gradient = adapter_scale * lax.dot_general(lowrank_output, prenorm_gradient, (((0,), (0,)), ((), ())), precision=highest_precision)
    return (keys, input_grad, down_grad, up_factor_gradient)

def reference(tokens, frozen_key_matrix, adapter_down_factor, adapter_up_factor, key_norm_gain, adapter_offset, loss_row_count, cotangent):
    blocks = N_DP * N_FSDP
    owner = jnp.broadcast_to(jnp.arange(N_FSDP, dtype=jnp.int32)[None, :], (N_DP, N_FSDP))
    global_ids = (owner * ADP_DEV + adapter_offset).reshape(-1).astype(jnp.int32)
    live_flat = loss_row_count.reshape(-1).astype(jnp.int32)
    totals = jnp.zeros((ADAPTER_COUNT,), jnp.int32).at[global_ids].add(live_flat)
    block_totals = totals[global_ids].astype(jnp.float32)
    token_blocks = tokens.reshape(blocks, BLOCK_ROWS, MODEL_WIDTH)
    cot_blocks = cotangent.reshape(blocks, BLOCK_ROWS, KEY_WINDOW_WIDTH)

    def per_block(accumulated, block_items):
        down_acc, up_acc = accumulated
        block_tokens, block_cot, adapter_number, live_count, adapter_total = block_items
        down_projection = lax.dynamic_index_in_dim(adapter_down_factor, adapter_number, 0, keepdims=False)
        up_projection = lax.dynamic_index_in_dim(adapter_up_factor, adapter_number, 0, keepdims=False)
        keys, input_grad, down_grad, up_factor_gradient = block_pass(block_tokens, frozen_key_matrix, down_projection, up_projection, key_norm_gain, live_count, adapter_total, block_cot)
        down_acc = lax.dynamic_update_index_in_dim(down_acc, lax.dynamic_index_in_dim(down_acc, adapter_number, 0, keepdims=False) + down_grad, adapter_number, 0)
        up_acc = lax.dynamic_update_index_in_dim(up_acc, lax.dynamic_index_in_dim(up_acc, adapter_number, 0, keepdims=False) + up_factor_gradient, adapter_number, 0)
        return ((down_acc, up_acc), (keys, input_grad))
    initial_carry = (jnp.zeros(adapter_down_factor.shape, jnp.float32), jnp.zeros(adapter_up_factor.shape, jnp.float32))
    (down_acc, up_acc), (all_keys, all_grads) = lax.scan(per_block, initial_carry, (token_blocks, cot_blocks, global_ids, live_flat, block_totals))
    return (all_keys.reshape(TOKENS, KEY_WINDOW_WIDTH), all_grads.reshape(TOKENS, MODEL_WIDTH), down_acc, up_acc)
```

```python
import functools

import jax
import jax.numpy as jnp
from jax import lax
from jax.experimental import pallas as pl
from jax.experimental.pallas import tpu as pltpu
from jax.sharding import PartitionSpec as P

HD = 128
SCALE = 2.0
EPS = 1e-06
NX, NYH, NZ = 4, 4, 8
NDP = NX * NYH
NFS = NZ * 4
RANK = 16
SLOTS = 3
BF, F32, I32 = jnp.bfloat16, jnp.float32, jnp.int32
HIGH = lax.Precision.HIGHEST
MINOR = (((1,), (1,)), ((), ()))
PLAIN = (((1,), (0,)), ((), ()))
EXCL = 96
FETCH = 256 - EXCL
HALF = FETCH // 2
XHALF = EXCL // 2


def dot(a, b, dims, precision=None):
    return lax.dot_general(a, b, dims, precision=precision, preferred_element_type=F32)


def split(v):
    hi = v.astype(BF)
    return hi, (v - hi.astype(F32)).astype(BF)


def kernel(
    off_ref, cnt_ref, gain_ref, down_ref, up_ref, cot_ref, tok_hbm, w_hbm,
    keys_ref, down_out, up_out, ig_hbm,
    wf, tok, ig, acc, pg, meta, msg_out, msg_in, gmsg_out, gmsg_in, upf, ups,
    loc_sem, ig_sem, zs, zr, ys, yr, xs, xr, ds_, dr, ms, mr, fs, fr, gs, gr,
):
    i, j = lax.axis_index("dp"), lax.axis_index("fsdp")
    yh, x = i // NX, i % NX
    z, yl, c = j // 4, (j // 2) % 2, j % 2
    px = x % 2

    def dp_of(a, b):
        return a * NX + b

    z_up = (i, (j + 4) % NFS)
    z_dn = (i, (j + NFS - 4) % NFS)
    sib = (i, j + 1 - 2 * c)
    jy = j + 2 - 4 * yl
    y_up = (dp_of((yh + yl) % NYH, x), jy)
    y_dn = (dp_of((yh + NYH - 1 + yl) % NYH, x), jy)
    x_up = (dp_of(yh, (x + 1) % NX), j)
    x_dn = (dp_of(yh, (x + NX - 1) % NX), j)

    def peer(r):
        return (i + r) % NDP

    tok_copy = pltpu.make_async_copy(tok_hbm, tok, loc_sem.at[0])
    tok_copy.start()
    pair_me = j // 2
    own = pltpu.make_async_copy(w_hbm, wf.at[pair_me, pl.ds(pl.multiple_of(256 * c, 256), 256)], loc_sem.at[1])
    own.start()

    off, cnt = off_ref[0, 0], cnt_ref[0, 0]
    rows8 = lax.broadcasted_iota(I32, (8, 128), 0)
    meta[i] = jnp.where(rows8 < 4, jnp.full((8, 128), off, I32), jnp.full((8, 128), cnt, I32))

    barrier = pltpu.get_barrier_semaphore()

    def greet(d):
        pl.semaphore_signal(barrier, inc=1, device_id=d, device_id_type=pl.DeviceIdType.MESH)

    for d in (z_up, z_dn, y_up, y_dn, sib):
        greet(d)

    @pl.loop(1, NDP)
    def _(r):
        greet((peer(r), j))

    pl.semaphore_wait(barrier, 5 + NDP - 1)

    def remote(src, dst, ssem, rsem, to):
        return pltpu.make_async_remote_copy(
            src_ref=src, dst_ref=dst, send_sem=ssem, recv_sem=rsem, device_id=to, device_id_type=pl.DeviceIdType.MESH
        )

    def rows(dz, par, start, size):
        zz = (z + dz + NZ) % NZ
        q = zz * 2 + (yl + par) % 2
        return wf.at[q, pl.ds(pl.multiple_of(256 * c + start, 16), size)]

    f0 = px * EXCL
    x0 = px * FETCH
    xo = (1 - px) * FETCH
    order = [(0, 0), (-1, 0), (1, 0), (0, 1), (-2, 0), (2, 0), (-1, 1), (1, 1),
             (-3, 0), (3, 0), (-2, 1), (2, 1), (4, 0), (-3, 1), (3, 1), (4, 1)]
    spot = {s: n for n, s in enumerate(order)}
    sends = []

    def send(src, ssem, rsem, to):
        copy = remote(src, src, ssem, rsem, to)
        copy.start()
        sends.append(copy)

    def arrived(ref, ssem, rsem):
        remote(ref, ref, ssem, rsem, sib).wait_recv()

    def z_piece(hop, dz):
        if hop < 4:
            return rows(dz, 0, f0, FETCH)
        return rows(dz, 0, f0 if dz < 0 else f0 + HALF, HALF)

    def send_z(hop):
        send(z_piece(hop, -(hop - 1) if hop < 4 else -3), zs.at[hop - 1], zr.at[hop - 1], z_up)
        send(z_piece(hop, hop - 1 if hop < 4 else 3), zs.at[3 + hop], zr.at[3 + hop], z_dn)

    def wait_z(hop):
        if hop < 4:
            arrived(rows(-hop, 0, f0, FETCH), zs.at[hop - 1], zr.at[hop - 1])
            arrived(rows(hop, 0, f0, FETCH), zs.at[3 + hop], zr.at[3 + hop])
        else:
            arrived(rows(4, 0, f0, HALF), zs.at[3], zr.at[3])
            arrived(rows(4, 0, f0 + HALF, HALF), zs.at[7], zr.at[7])

    def send_y(dz):
        n = 2 * (dz + 3)
        send(rows(dz, 0, f0, HALF), ys.at[n], yr.at[n], y_up)
        send(rows(dz, 0, f0 + HALF, HALF), ys.at[n + 1], yr.at[n + 1], y_dn)

    def wait_y(dz):
        n = 2 * (dz + 3)
        arrived(rows(dz, 1, f0, HALF), ys.at[n], yr.at[n])
        arrived(rows(dz, 1, f0 + HALF, HALF), ys.at[n + 1], yr.at[n + 1])

    def send_x(dz, par):
        n = 2 * spot[dz, par]
        send(rows(dz, par, x0, XHALF), xs.at[n], xr.at[n], x_up)
        send(rows(dz, par, x0 + XHALF, XHALF), xs.at[n + 1], xr.at[n + 1], x_dn)

    def wait_x(dz, par):
        n = 2 * spot[dz, par]
        arrived(rows(dz, par, xo, XHALF), xs.at[n], xr.at[n])
        arrived(rows(dz, par, xo + XHALF, XHALF), xs.at[n + 1], xr.at[n + 1])

    def send_d(dz, par):
        n = spot[dz, par]
        send(rows(dz, par, 0, 256), ds_.at[n], dr.at[n], sib)

    def wait_d(dz, par):
        n = spot[dz, par]
        zz = (z + dz + NZ) % NZ
        q = zz * 2 + (yl + par) % 2
        ref = wf.at[q, pl.ds(pl.multiple_of(256 * (1 - c), 256), 256)]
        arrived(ref, ds_.at[n], dr.at[n])
        return q

    own.wait()
    send_z(1)
    send_y(0)
    send_d(0, 0)

    @pl.loop(1, NDP)
    def _(r):
        remote(meta.at[i], meta.at[i], ms.at[r], mr.at[r], (peer(r), j)).start()

    acc[...] = jnp.zeros_like(acc)
    ups[...] = jnp.zeros_like(ups)
    ups[:, :, 0:32] = up_ref[...]
    quarter = i % 4

    def placed(v):
        out = v
        for n in range(1, 4):
            out = jnp.where(quarter == n, pltpu.roll(v, 32 * n, 1), out)
        return out

    for s in range(SLOTS):
        ups[s] = placed(ups[s])

    @pl.loop(1, NDP)
    def _(r):
        from_ = (i + NDP - r) % NDP
        remote(meta.at[from_], meta.at[from_], ms.at[r], mr.at[r], sib).wait_recv()

    def chosen(o, width, ref):
        o = jnp.broadcast_to(o[0:1, 0:1], (RANK, width))
        return jnp.where(o == 0, ref[0], jnp.where(o == 1, ref[1], ref[2]))

    def build(p, dst):
        o = meta[p]
        dst[:, 0:512] = chosen(o, 512, down_ref).astype(BF)
        hi, lo = split(chosen(o, 128, ups))
        dst[:, 512:640] = hi
        dst[:, 640:768] = lo

    build(i, msg_in.at[i])

    @pl.loop(1, NDP)
    def _(r):
        p = peer(r)
        build(p, msg_out.at[p])
        remote(msg_out.at[p], msg_in.at[i], fs.at[r], fr.at[r], (p, j)).start()

    def product(q):
        cols = pl.ds(pl.multiple_of(512 * q, 512), 512)
        acc[...] += dot(tok[:, cols], wf[q], PLAIN)

    tok_copy.wait()

    wait_z(1)
    send_z(2)
    send_y(-1)
    send_y(1)
    send_x(-1, 0)
    send_x(1, 0)
    wait_y(0)
    send_x(0, 1)
    product(wait_d(0, 0))
    wait_z(2)
    send_z(3)
    send_y(-2)
    send_y(2)
    send_x(-2, 0)
    send_x(2, 0)
    wait_x(-1, 0)
    send_d(-1, 0)
    wait_x(1, 0)
    send_d(1, 0)
    wait_y(-1)
    send_x(-1, 1)
    wait_y(1)
    send_x(1, 1)
    wait_x(0, 1)
    send_d(0, 1)
    wait_z(3)
    send_z(4)
    send_y(-3)
    send_y(3)
    send_x(-3, 0)
    send_x(3, 0)
    wait_x(-2, 0)
    send_d(-2, 0)
    wait_x(2, 0)
    send_d(2, 0)
    wait_y(-2)
    send_x(-2, 1)
    wait_y(2)
    send_x(2, 1)
    wait_x(-1, 1)
    send_d(-1, 1)
    wait_x(1, 1)
    send_d(1, 1)
    product(wait_d(-1, 0))
    product(wait_d(1, 0))
    product(wait_d(0, 1))
    wait_z(4)
    send_y(4)
    send_x(4, 0)
    wait_x(-3, 0)
    send_d(-3, 0)
    wait_x(3, 0)
    send_d(3, 0)
    wait_y(-3)
    send_x(-3, 1)
    wait_y(3)
    send_x(3, 1)
    wait_x(-2, 1)
    send_d(-2, 1)
    wait_x(2, 1)
    send_d(2, 1)

    @pl.loop(1, NDP)
    def _(r):
        from_ = (i + NDP - r) % NDP
        remote(msg_in.at[from_], msg_in.at[from_], fs.at[r], fr.at[r], sib).wait_recv()

    def low(p, total):
        cols = pl.ds(pl.multiple_of(512 * p, 512), 512)
        return total + dot(msg_in[p, :, 0:512], tok[:, cols], MINOR)

    lr_t = lax.fori_loop(0, NDP, low, jnp.zeros((RANK, 128), F32))
    for h in range(4):
        total = jnp.zeros((RANK, 128), F32)
        for q in range(4):
            total += msg_in[4 * h + q, :, 512:640].astype(F32) + msg_in[4 * h + q, :, 640:768].astype(F32)
        upf[:, 128 * h : 128 * h + 128] = total
    up = upf[...]

    wait_y(4)
    send_x(4, 1)
    wait_x(4, 0)
    send_d(4, 0)
    wait_x(-3, 1)
    send_d(-3, 1)
    wait_x(3, 1)
    send_d(3, 1)
    for s in ((-2, 0), (2, 0), (-1, 1), (1, 1)):
        product(wait_d(*s))
    for s in ((-3, 0), (3, 0), (-2, 1), (2, 1)):
        product(wait_d(*s))
    extra = SCALE * dot(lr_t.T, up, PLAIN, HIGH)
    wait_x(4, 1)
    send_d(4, 1)
    for s in ((4, 0), (-3, 1), (3, 1), (4, 1)):
        product(wait_d(*s))

    offs, cnts = meta[:, 0, :], meta[:, 4, :]
    total = jnp.sum(jnp.where(offs == off, cnts, 0), axis=0, keepdims=True).astype(F32)
    live = lax.broadcasted_iota(I32, (128, 128), 0) < cnt
    row_scale = jnp.where(live, jnp.broadcast_to(128.0 / total, (128, 128)), 0.0)
    gain = gain_ref[...]
    for h in range(4):
        cols = slice(128 * h, 128 * h + 128)
        projected = acc[:, cols] + extra[:, cols]
        inverse = lax.rsqrt(jnp.mean(projected * projected, axis=-1, keepdims=True) + EPS)
        normed = projected * inverse
        keys_ref[:, cols] = (normed * gain).astype(BF)
        scaled = cot_ref[:, cols].astype(F32) * row_scale * gain
        along = jnp.mean(scaled * normed, axis=-1, keepdims=True)
        pg[:, cols] = inverse * (scaled - normed * along)
    pre = pg[...]
    pre_low = pre.astype(BF)
    lg_t = SCALE * dot(up, pre, MINOR, HIGH)
    hi, lo = split(lg_t)
    lg_t2 = jnp.concatenate([hi, lo], axis=0)
    lg2 = jnp.concatenate([hi.astype(F32), lo.astype(F32)], axis=0).T.astype(BF)
    upg = SCALE * dot(lr_t, pre, PLAIN, HIGH)
    upf[...] = upg

    def grads(p, dst):
        cols = pl.ds(pl.multiple_of(512 * p, 512), 512)
        both = dot(lg_t2, tok[:, cols], PLAIN)
        dst[:, 0:512] = (both[0:RANK] + both[RANK:]).astype(BF)
        hi, lo = split(upf[:, pl.ds(pl.multiple_of(128 * (p // 4), 128), 128)])
        dst[:, 512:640] = hi
        dst[:, 640:768] = lo

    @pl.loop(1, NDP)
    def _(r):
        p = peer(r)
        grads(p, gmsg_out.at[p])
        remote(gmsg_out.at[p], gmsg_in.at[i], gs.at[r], gr.at[r], (p, j)).start()

    grads(i, gmsg_in.at[i])

    def ig_copy(q):
        cols = pl.ds(pl.multiple_of(512 * q, 512), 512)
        return pltpu.make_async_copy(ig.at[:, cols], ig_hbm.at[:, cols], ig_sem.at[q])

    @pl.loop(0, NFS // 2)
    def _(q):
        cols = pl.ds(pl.multiple_of(512 * q, 512), 512)
        d = msg_in[q, :, 0:512]
        part = dot(lg2, jnp.concatenate([d, d], axis=0), PLAIN)
        ig[:, cols] = (part + dot(pre_low, wf[q], MINOR)).astype(BF)
        ig_copy(q).start()

    def gather(p, sums):
        o = jnp.broadcast_to(meta[p][0:1, 0:1], (RANK, 512))
        ou = o[:, 0:128]
        d = gmsg_in[p, :, 0:512].astype(F32)
        u = gmsg_in[p, :, 512:640].astype(F32) + gmsg_in[p, :, 640:768].astype(F32)
        return tuple(
            (sd + jnp.where(o == s, d, 0.0), su + jnp.where(ou == s, u, 0.0)) for s, (sd, su) in enumerate(sums)
        )

    zero = (jnp.zeros((RANK, 512), F32), jnp.zeros((RANK, 128), F32))
    sums = gather(i, (zero,) * SLOTS)

    def later(r, sums):
        from_ = (i + NDP - r) % NDP
        remote(gmsg_in.at[from_], gmsg_in.at[from_], gs.at[r], gr.at[r], sib).wait_recv()
        return gather(from_, sums)

    sums = lax.fori_loop(1, NDP, later, sums)
    for s, (sd, su) in enumerate(sums):
        down_out[s] = sd
        mine = su
        for n in range(1, 4):
            mine = jnp.where(quarter == n, pltpu.roll(su, 128 - 32 * n, 1), mine)
        up_out[s] = mine[:, 0:32]

    for copy in sends:
        copy.wait_send()

    @pl.loop(1, NDP)
    def _(r):
        p = peer(r)
        remote(meta.at[i], meta.at[i], ms.at[r], mr.at[r], (p, j)).wait_send()
        remote(msg_out.at[p], msg_in.at[i], fs.at[r], fr.at[r], (p, j)).wait_send()
        remote(gmsg_out.at[p], gmsg_in.at[i], gs.at[r], gr.at[r], (p, j)).wait_send()

    @pl.loop(0, NFS // 2)
    def _(q):
        ig_copy(q).wait()


def on_device(tokens, weight, down, up, gain, offset, count, cot):
    n_rows, width = tokens.shape
    keys = cot.shape[1]
    vmem = pl.BlockSpec(memory_space=pltpu.VMEM)
    smem = pl.BlockSpec(memory_space=pltpu.SMEM)
    anywhere = pl.BlockSpec(memory_space=pl.ANY)
    dma = pltpu.SemaphoreType.DMA
    down_t = jnp.transpose(down, (0, 2, 1))
    out = pl.pallas_call(
        kernel,
        out_shape=(
            jax.ShapeDtypeStruct((n_rows, keys), BF),
            jax.ShapeDtypeStruct(down_t.shape, F32),
            jax.ShapeDtypeStruct(up.shape, F32),
            jax.ShapeDtypeStruct((n_rows, width), BF),
        ),
        in_specs=[smem, smem, vmem, vmem, vmem, vmem, anywhere, anywhere],
        out_specs=(vmem, vmem, vmem, anywhere),
        scratch_shapes=[
            pltpu.VMEM((NFS // 2, 512, keys), BF),
            pltpu.VMEM((n_rows, width), BF),
            pltpu.VMEM((n_rows, width), BF),
            pltpu.VMEM((n_rows, keys), F32),
            pltpu.VMEM((n_rows, keys), F32),
            pltpu.VMEM((NDP, 8, 128), I32),
            pltpu.VMEM((NDP, RANK, 768), BF),
            pltpu.VMEM((NDP, RANK, 768), BF),
            pltpu.VMEM((NDP, RANK, 768), BF),
            pltpu.VMEM((NDP, RANK, 768), BF),
            pltpu.VMEM((RANK, keys), F32),
            pltpu.VMEM((SLOTS, RANK, 128), F32),
            dma((2,)), dma((16,)),
            dma((8,)), dma((8,)),
            dma((16,)), dma((16,)),
            dma((32,)), dma((32,)),
            dma((16,)), dma((16,)),
            dma((16,)), dma((16,)),
            dma((16,)), dma((16,)),
            dma((16,)), dma((16,)),
        ],
        compiler_params=pltpu.CompilerParams(
            collective_id=0, has_side_effects=True, vmem_limit_bytes=40 * 1024 * 1024
        ),
        name="key_projection",
    )(offset, count, gain.reshape(1, HD), down_t, up, cot, tokens, weight)
    keys_out, down_grad, up_grad, input_grad = out
    return keys_out, input_grad, jnp.transpose(down_grad, (0, 2, 1)), up_grad


def solution(mesh):
    rows = P(("dp", "fsdp"), None)
    down, up, cell = P("fsdp", "dp", None), P("fsdp", None, "dp"), P("dp", "fsdp")
    return jax.shard_map(
        on_device,
        mesh=mesh,
        in_specs=(rows, P("fsdp", None), down, up, P(), cell, cell, rows),
        out_specs=(rows, rows, down, up),
        check_vma=False,
    )
```

```python
import functools

import jax
import jax.numpy as jnp
from jax import lax
from jax.experimental import pallas as pl
from jax.experimental.pallas import tpu as pltpu
from jax.sharding import PartitionSpec as P

HD = 128
SCALE = 2.0
EPS = 1e-06
NX, NYH, NZ = 4, 4, 8
NDP = NX * NYH
NFS = NZ * 4
RANK = 16
SLOTS = 3
BF, F32, I32 = jnp.bfloat16, jnp.float32, jnp.int32
HIGH = lax.Precision.HIGHEST
MINOR = (((1,), (1,)), ((), ()))
PLAIN = (((1,), (0,)), ((), ()))
EXCL = 96
FETCH = 256 - EXCL
HALF = FETCH // 2
XHALF = EXCL // 2


def dot(a, b, dims, precision=None):
    return lax.dot_general(a, b, dims, precision=precision, preferred_element_type=F32)


def split(v):
    hi = v.astype(BF)
    return hi, (v - hi.astype(F32)).astype(BF)


def kernel(
    off_ref, cnt_ref, gain_hbm, down_hbm, up_hbm, cot_hbm, tok_hbm, w_hbm,
    keys_ref, down_out, up_out, ig,
    gain_ref, down_ref, up_ref, cot_ref, wf, tok, acc, pg, meta, msg_out, msg_in, gmsg_out, gmsg_in, upf, ups,
    loc_sem, zs, zr, ys, yr, xs, xr, ds_, dr, ms, mr, fs, fr, gs, gr,
):
    i, j = lax.axis_index("dp"), lax.axis_index("fsdp")
    yh, x = i // NX, i % NX
    z, yl, c = j // 4, (j // 2) % 2, j % 2
    px = x % 2

    def dp_of(a, b):
        return a * NX + b

    z_up = (i, (j + 4) % NFS)
    z_dn = (i, (j + NFS - 4) % NFS)
    sib = (i, j + 1 - 2 * c)
    jy = j + 2 - 4 * yl
    y_up = (dp_of((yh + yl) % NYH, x), jy)
    y_dn = (dp_of((yh + NYH - 1 + yl) % NYH, x), jy)
    x_up = (dp_of(yh, (x + 1) % NX), j)
    x_dn = (dp_of(yh, (x + NX - 1) % NX), j)

    def peer(r):
        return (i + r) % NDP

    pair_me = j // 2
    local = [
        pltpu.make_async_copy(src, dst, loc_sem.at[n])
        for n, (src, dst) in enumerate((
            (w_hbm, wf.at[pair_me, pl.ds(pl.multiple_of(256 * c, 256), 256)]),
            (down_hbm, down_ref),
            (up_hbm, up_ref),
            (tok_hbm, tok),
            (gain_hbm, gain_ref),
            (cot_hbm, cot_ref),
        ))
    ]
    for copy in local:
        copy.start()
    own = local[0]
    off, cnt = off_ref[0, 0], cnt_ref[0, 0]
    rows8 = lax.broadcasted_iota(I32, (8, 128), 0)
    meta[i] = jnp.where(rows8 < 4, jnp.full((8, 128), off, I32), jnp.full((8, 128), cnt, I32))

    barrier = pltpu.get_barrier_semaphore()

    def greet(d):
        pl.semaphore_signal(barrier, inc=1, device_id=d, device_id_type=pl.DeviceIdType.MESH)

    for d in (z_up, z_dn, y_up, y_dn, sib):
        greet(d)

    @pl.loop(1, NDP)
    def _(r):
        greet((peer(r), j))

    pl.semaphore_wait(barrier, 5 + NDP - 1)

    def remote(src, dst, ssem, rsem, to):
        return pltpu.make_async_remote_copy(
            src_ref=src, dst_ref=dst, send_sem=ssem, recv_sem=rsem, device_id=to, device_id_type=pl.DeviceIdType.MESH
        )

    def rows(dz, par, start, size):
        zz = (z + dz + NZ) % NZ
        q = zz * 2 + (yl + par) % 2
        return wf.at[q, pl.ds(pl.multiple_of(256 * c + start, 16), size)]

    f0 = px * EXCL
    x0 = px * FETCH
    xo = (1 - px) * FETCH
    order = [(0, 0), (-1, 0), (1, 0), (0, 1), (-2, 0), (2, 0), (-1, 1), (1, 1),
             (-3, 0), (3, 0), (-2, 1), (2, 1), (4, 0), (-3, 1), (3, 1), (4, 1)]
    spot = {s: n for n, s in enumerate(order)}
    sends = []

    def send(src, ssem, rsem, to):
        copy = remote(src, src, ssem, rsem, to)
        copy.start()
        sends.append(copy)

    def arrived(ref, ssem, rsem):
        remote(ref, ref, ssem, rsem, sib).wait_recv()

    def z_piece(hop, dz):
        if hop < 4:
            return rows(dz, 0, f0, FETCH)
        return rows(dz, 0, f0 if dz < 0 else f0 + HALF, HALF)

    def send_z(hop):
        send(z_piece(hop, -(hop - 1) if hop < 4 else -3), zs.at[hop - 1], zr.at[hop - 1], z_up)
        send(z_piece(hop, hop - 1 if hop < 4 else 3), zs.at[3 + hop], zr.at[3 + hop], z_dn)

    def wait_z(hop):
        if hop < 4:
            arrived(rows(-hop, 0, f0, FETCH), zs.at[hop - 1], zr.at[hop - 1])
            arrived(rows(hop, 0, f0, FETCH), zs.at[3 + hop], zr.at[3 + hop])
        else:
            arrived(rows(4, 0, f0, HALF), zs.at[3], zr.at[3])
            arrived(rows(4, 0, f0 + HALF, HALF), zs.at[7], zr.at[7])

    def send_y(dz):
        n = 2 * (dz + 3)
        send(rows(dz, 0, f0, HALF), ys.at[n], yr.at[n], y_up)
        send(rows(dz, 0, f0 + HALF, HALF), ys.at[n + 1], yr.at[n + 1], y_dn)

    def wait_y(dz):
        n = 2 * (dz + 3)
        arrived(rows(dz, 1, f0, HALF), ys.at[n], yr.at[n])
        arrived(rows(dz, 1, f0 + HALF, HALF), ys.at[n + 1], yr.at[n + 1])

    def send_x(dz, par):
        n = 2 * spot[dz, par]
        send(rows(dz, par, x0, XHALF), xs.at[n], xr.at[n], x_up)
        send(rows(dz, par, x0 + XHALF, XHALF), xs.at[n + 1], xr.at[n + 1], x_dn)

    def wait_x(dz, par):
        n = 2 * spot[dz, par]
        arrived(rows(dz, par, xo, XHALF), xs.at[n], xr.at[n])
        arrived(rows(dz, par, xo + XHALF, XHALF), xs.at[n + 1], xr.at[n + 1])

    def send_d(dz, par):
        n = spot[dz, par]
        send(rows(dz, par, 0, 256), ds_.at[n], dr.at[n], sib)

    def wait_d(dz, par):
        n = spot[dz, par]
        zz = (z + dz + NZ) % NZ
        q = zz * 2 + (yl + par) % 2
        ref = wf.at[q, pl.ds(pl.multiple_of(256 * (1 - c), 256), 256)]
        arrived(ref, ds_.at[n], dr.at[n])
        return q

    own.wait()
    send_z(1)
    send_y(0)
    send_d(0, 0)

    @pl.loop(1, NDP)
    def _(r):
        remote(meta.at[i], meta.at[i], ms.at[r], mr.at[r], (peer(r), j)).start()

    acc[...] = jnp.zeros_like(acc)
    ups[...] = jnp.zeros_like(ups)
    local[2].wait()
    ups[:, :, 0:32] = up_ref[...]
    quarter = i % 4

    def placed(v):
        out = v
        for n in range(1, 4):
            out = jnp.where(quarter == n, pltpu.roll(v, 32 * n, 1), out)
        return out

    for s in range(SLOTS):
        ups[s] = placed(ups[s])

    @pl.loop(1, NDP)
    def _(r):
        from_ = (i + NDP - r) % NDP
        remote(meta.at[from_], meta.at[from_], ms.at[r], mr.at[r], sib).wait_recv()

    def chosen(o, width, ref):
        o = jnp.broadcast_to(o[0:1, 0:1], (RANK, width))
        return jnp.where(o == 0, ref[0], jnp.where(o == 1, ref[1], ref[2]))

    def build(p, dst):
        o = meta[p]
        dst[:, 0:512] = chosen(o, 512, down_ref).astype(BF)
        hi, lo = split(chosen(o, 128, ups))
        dst[:, 512:640] = hi
        dst[:, 640:768] = lo

    local[1].wait()
    build(i, msg_in.at[i])

    @pl.loop(1, NDP)
    def _(r):
        p = peer(r)
        build(p, msg_out.at[p])
        remote(msg_out.at[p], msg_in.at[i], fs.at[r], fr.at[r], (p, j)).start()

    def product(q):
        cols = pl.ds(pl.multiple_of(512 * q, 512), 512)
        acc[...] += dot(tok[:, cols], wf[q], PLAIN)

    for copy in local[3:]:
        copy.wait()

    wait_z(1)
    send_z(2)
    send_y(-1)
    send_y(1)
    send_x(-1, 0)
    send_x(1, 0)
    wait_y(0)
    send_x(0, 1)
    product(wait_d(0, 0))
    wait_z(2)
    send_z(3)
    send_y(-2)
    send_y(2)
    send_x(-2, 0)
    send_x(2, 0)
    wait_x(-1, 0)
    send_d(-1, 0)
    wait_x(1, 0)
    send_d(1, 0)
    wait_y(-1)
    send_x(-1, 1)
    wait_y(1)
    send_x(1, 1)
    wait_x(0, 1)
    send_d(0, 1)
    wait_z(3)
    send_z(4)
    send_y(-3)
    send_y(3)
    send_x(-3, 0)
    send_x(3, 0)
    wait_x(-2, 0)
    send_d(-2, 0)
    wait_x(2, 0)
    send_d(2, 0)
    wait_y(-2)
    send_x(-2, 1)
    wait_y(2)
    send_x(2, 1)
    wait_x(-1, 1)
    send_d(-1, 1)
    wait_x(1, 1)
    send_d(1, 1)
    product(wait_d(-1, 0))
    product(wait_d(1, 0))
    product(wait_d(0, 1))
    wait_z(4)
    send_y(4)
    send_x(4, 0)
    wait_x(-3, 0)
    send_d(-3, 0)
    wait_x(3, 0)
    send_d(3, 0)
    wait_y(-3)
    send_x(-3, 1)
    wait_y(3)
    send_x(3, 1)
    wait_x(-2, 1)
    send_d(-2, 1)
    wait_x(2, 1)
    send_d(2, 1)

    @pl.loop(1, NDP)
    def _(r):
        from_ = (i + NDP - r) % NDP
        remote(msg_in.at[from_], msg_in.at[from_], fs.at[r], fr.at[r], sib).wait_recv()

    def low(p, total):
        cols = pl.ds(pl.multiple_of(512 * p, 512), 512)
        return total + dot(msg_in[p, :, 0:512], tok[:, cols], MINOR)

    lr_t = lax.fori_loop(0, NDP, low, jnp.zeros((RANK, 128), F32))
    for h in range(4):
        total = jnp.zeros((RANK, 128), F32)
        for q in range(4):
            total += msg_in[4 * h + q, :, 512:640].astype(F32) + msg_in[4 * h + q, :, 640:768].astype(F32)
        upf[:, 128 * h : 128 * h + 128] = total
    up = upf[...]

    wait_y(4)
    send_x(4, 1)
    wait_x(4, 0)
    send_d(4, 0)
    wait_x(-3, 1)
    send_d(-3, 1)
    wait_x(3, 1)
    send_d(3, 1)
    for s in ((-2, 0), (2, 0), (-1, 1), (1, 1)):
        product(wait_d(*s))
    for s in ((-3, 0), (3, 0), (-2, 1), (2, 1)):
        product(wait_d(*s))
    extra = SCALE * dot(lr_t.T, up, PLAIN, HIGH)
    wait_x(4, 1)
    send_d(4, 1)
    for s in ((4, 0), (-3, 1), (3, 1), (4, 1)):
        product(wait_d(*s))

    offs, cnts = meta[:, 0, :], meta[:, 4, :]
    total = jnp.sum(jnp.where(offs == off, cnts, 0), axis=0, keepdims=True).astype(F32)
    live = lax.broadcasted_iota(I32, (128, 128), 0) < cnt
    row_scale = jnp.where(live, jnp.broadcast_to(128.0 / total, (128, 128)), 0.0)
    gain = gain_ref[...]
    for h in range(4):
        cols = slice(128 * h, 128 * h + 128)
        projected = acc[:, cols] + extra[:, cols]
        inverse = lax.rsqrt(jnp.mean(projected * projected, axis=-1, keepdims=True) + EPS)
        normed = projected * inverse
        keys_ref[:, cols] = (normed * gain).astype(BF)
        scaled = cot_ref[:, cols].astype(F32) * row_scale * gain
        along = jnp.mean(scaled * normed, axis=-1, keepdims=True)
        pg[:, cols] = inverse * (scaled - normed * along)
    pre = pg[...]
    pre_low = pre.astype(BF)
    lg_t = SCALE * dot(up, pre, MINOR, HIGH)
    hi, lo = split(lg_t)
    lg_t2 = jnp.concatenate([hi, lo], axis=0)
    lg2 = jnp.concatenate([hi.astype(F32), lo.astype(F32)], axis=0).T.astype(BF)
    upg = SCALE * dot(lr_t, pre, PLAIN, HIGH)
    upf[...] = upg

    def grads(p, dst):
        cols = pl.ds(pl.multiple_of(512 * p, 512), 512)
        both = dot(lg_t2, tok[:, cols], PLAIN)
        dst[:, 0:512] = (both[0:RANK] + both[RANK:]).astype(BF)
        hi, lo = split(upf[:, pl.ds(pl.multiple_of(128 * (p // 4), 128), 128)])
        dst[:, 512:640] = hi
        dst[:, 640:768] = lo

    @pl.loop(1, NDP)
    def _(r):
        p = peer(r)
        grads(p, gmsg_out.at[p])
        remote(gmsg_out.at[p], gmsg_in.at[i], gs.at[r], gr.at[r], (p, j)).start()

    grads(i, gmsg_in.at[i])

    @pl.loop(0, NFS // 2)
    def _(q):
        cols = pl.ds(pl.multiple_of(512 * q, 512), 512)
        d = msg_in[q, :, 0:512]
        part = dot(lg2, jnp.concatenate([d, d], axis=0), PLAIN)
        ig[:, cols] = (part + dot(pre_low, wf[q], MINOR)).astype(BF)

    def gather(p, sums):
        o = jnp.broadcast_to(meta[p][0:1, 0:1], (RANK, 512))
        ou = o[:, 0:128]
        d = gmsg_in[p, :, 0:512].astype(F32)
        u = gmsg_in[p, :, 512:640].astype(F32) + gmsg_in[p, :, 640:768].astype(F32)
        return tuple(
            (sd + jnp.where(o == s, d, 0.0), su + jnp.where(ou == s, u, 0.0)) for s, (sd, su) in enumerate(sums)
        )

    zero = (jnp.zeros((RANK, 512), F32), jnp.zeros((RANK, 128), F32))
    sums = gather(i, (zero,) * SLOTS)

    def later(r, sums):
        from_ = (i + NDP - r) % NDP
        remote(gmsg_in.at[from_], gmsg_in.at[from_], gs.at[r], gr.at[r], sib).wait_recv()
        return gather(from_, sums)

    sums = lax.fori_loop(1, NDP, later, sums)
    for s, (sd, su) in enumerate(sums):
        down_out[s] = sd
        mine = su
        for n in range(1, 4):
            mine = jnp.where(quarter == n, pltpu.roll(su, 128 - 32 * n, 1), mine)
        up_out[s] = mine[:, 0:32]

    for copy in sends:
        copy.wait_send()

    @pl.loop(1, NDP)
    def _(r):
        p = peer(r)
        remote(meta.at[i], meta.at[i], ms.at[r], mr.at[r], (p, j)).wait_send()
        remote(msg_out.at[p], msg_in.at[i], fs.at[r], fr.at[r], (p, j)).wait_send()
        remote(gmsg_out.at[p], gmsg_in.at[i], gs.at[r], gr.at[r], (p, j)).wait_send()


def put_kernel(*refs):
    n = len(refs) // 2
    sem = refs[-1]
    copies = []
    for src, dst in zip(refs[:n], refs[n : 2 * n], strict=True):
        rows = src.shape[0]
        parts = 8 if rows == 128 and src.shape[1] > 1024 else 1
        for k in range(parts):
            cut = pl.ds(k * (rows // parts), rows // parts)
            copies.append(pltpu.make_async_copy(src.at[cut], dst.at[cut], sem.at[len(copies)]))
    for copy in copies:
        copy.start()
    for copy in copies:
        copy.wait()


def put(*arrays):
    hbm = pl.BlockSpec(memory_space=pltpu.MemorySpace.HBM)
    return pl.pallas_call(
        put_kernel,
        out_shape=tuple(jax.ShapeDtypeStruct(a.shape, a.dtype) for a in arrays),
        in_specs=[pl.BlockSpec(memory_space=pltpu.VMEM)] * len(arrays),
        out_specs=(hbm,) * len(arrays),
        scratch_shapes=[pltpu.SemaphoreType.DMA((16,))],
        name="put",
    )(*(pltpu.with_memory_space_constraint(a, pltpu.MemorySpace.VMEM) for a in arrays))


def stay(a):
    return pltpu.with_memory_space_constraint(a, pltpu.MemorySpace.HBM)


def on_device(tokens, weight, down, up, gain, offset, count, cot):
    n_rows, width = tokens.shape
    keys = cot.shape[1]
    vmem = pl.BlockSpec(memory_space=pltpu.VMEM)
    smem = pl.BlockSpec(memory_space=pltpu.SMEM)
    hbm = pl.BlockSpec(memory_space=pltpu.MemorySpace.HBM)
    dma = pltpu.SemaphoreType.DMA
    down_t = jnp.transpose(down, (0, 2, 1))
    out = pl.pallas_call(
        kernel,
        out_shape=(
            pltpu.VMEM((n_rows, keys), BF),
            pltpu.VMEM(down_t.shape, F32),
            pltpu.VMEM(up.shape, F32),
            pltpu.VMEM((n_rows, width), BF),
        ),
        in_specs=[smem] * 2 + [hbm] * 6,
        out_specs=(vmem,) * 4,
        scratch_shapes=[
            pltpu.VMEM((1, HD), F32),
            pltpu.VMEM(down_t.shape, F32),
            pltpu.VMEM(up.shape, F32),
            pltpu.VMEM((n_rows, keys), BF),
            pltpu.VMEM((NFS // 2, 512, keys), BF),
            pltpu.VMEM((n_rows, width), BF),
            pltpu.VMEM((n_rows, keys), F32),
            pltpu.VMEM((n_rows, keys), F32),
            pltpu.VMEM((NDP, 8, 128), I32),
            pltpu.VMEM((NDP, RANK, 768), BF),
            pltpu.VMEM((NDP, RANK, 768), BF),
            pltpu.VMEM((NDP, RANK, 768), BF),
            pltpu.VMEM((NDP, RANK, 768), BF),
            pltpu.VMEM((RANK, keys), F32),
            pltpu.VMEM((SLOTS, RANK, 128), F32),
            dma((8,)),
            dma((8,)), dma((8,)),
            dma((16,)), dma((16,)),
            dma((32,)), dma((32,)),
            dma((16,)), dma((16,)),
            dma((16,)), dma((16,)),
            dma((16,)), dma((16,)),
            dma((16,)), dma((16,)),
        ],
        compiler_params=pltpu.CompilerParams(
            collective_id=0, has_side_effects=True, vmem_limit_bytes=40 * 1024 * 1024
        ),
        name="key_projection",
    )(offset, count, *(stay(a) for a in (gain.reshape(1, HD), down_t, up, cot, tokens, weight)))
    keys_out, down_grad, up_grad, input_grad = put(*out)
    return keys_out, input_grad, jnp.transpose(down_grad, (0, 2, 1)), up_grad


def solution(mesh):
    rows = P(("dp", "fsdp"), None)
    down, up, cell = P("fsdp", "dp", None), P("fsdp", None, "dp"), P("dp", "fsdp")
    return jax.shard_map(
        on_device,
        mesh=mesh,
        in_specs=(rows, P("fsdp", None), down, up, P(), cell, cell, rows),
        out_specs=(rows, rows, down, up),
        check_vma=False,
    )
```

```python
import functools

import jax
import jax.numpy as jnp
from jax import lax
from jax.experimental import pallas as pl
from jax.experimental.pallas import tpu as pltpu
from jax.sharding import PartitionSpec as P

HD = 128
SCALE = 2.0
EPS = 1e-06
NX, NYH, NZ = 4, 4, 8
NDP = NX * NYH
NFS = NZ * 4
RANK = 16
SLOTS = 3
BF, F32, I32 = jnp.bfloat16, jnp.float32, jnp.int32
MINOR = (((1,), (1,)), ((), ()))
PLAIN = (((1,), (0,)), ((), ()))
EXCL = 96
FETCH = 256 - EXCL
HALF = FETCH // 2
XHALF = EXCL // 2


ORDER = ((8, 12), (4, 8), (12, 16), (1, 4))


def dot(a, b, dims, precision=None):
    return lax.dot_general(a, b, dims, precision=precision, preferred_element_type=F32)


def split(v):
    hi = v.astype(BF)
    return hi, (v - hi.astype(F32)).astype(BF)


def kernel(
    off_ref, cnt_ref, gain_hbm, down_hbm, up_hbm, cot_hbm, tok_hbm, w_hbm,
    keys_ref, down_out, up_out, ig,
    gain_ref, down_ref, up_ref, cot_ref, wf, tok, acc, pg, meta, msg_out, msg_in, gmsg_out, gmsg_in, upf, ups,
    loc_sem, zs, zr, ys, yr, xs, xr, ds_, dr, ms, mr, fs, fr, gs, gr,
):
    i, j = lax.axis_index("dp"), lax.axis_index("fsdp")
    yh, x = i // NX, i % NX
    z, yl, c = j // 4, (j // 2) % 2, j % 2
    px = x % 2

    def dp_of(a, b):
        return a * NX + b

    z_up = (i, (j + 4) % NFS)
    z_dn = (i, (j + NFS - 4) % NFS)
    sib = (i, j + 1 - 2 * c)
    jy = j + 2 - 4 * yl
    y_up = (dp_of((yh + yl) % NYH, x), jy)
    y_dn = (dp_of((yh + NYH - 1 + yl) % NYH, x), jy)
    x_up = (dp_of(yh, (x + 1) % NX), j)
    x_dn = (dp_of(yh, (x + NX - 1) % NX), j)

    def peer(r):
        return dp_of((yh + r // NX) % NYH, (x + r % NX) % NX)

    def source(r):
        return dp_of((yh + NYH - r // NX) % NYH, (x + NX - r % NX) % NX)

    def loops(who):
        def run(body):
            for first, last in ORDER:
                pl.loop(first, last)(lambda r: body(r, who(r)))
        return run

    each, each_from = loops(peer), loops(source)

    pair_me = j // 2
    local = [
        pltpu.make_async_copy(src, dst, loc_sem.at[n])
        for n, (src, dst) in enumerate((
            (w_hbm, wf.at[pair_me, pl.ds(pl.multiple_of(256 * c, 256), 256)]),
            (down_hbm, down_ref),
            (up_hbm, up_ref),
            (tok_hbm, tok),
            (gain_hbm, gain_ref),
            (cot_hbm, cot_ref),
        ))
    ]
    for copy in local:
        copy.start()
    own = local[0]
    off, cnt = off_ref[0, 0], cnt_ref[0, 0]
    rows8 = lax.broadcasted_iota(I32, (8, 128), 0)
    meta[i] = jnp.where(rows8 < 4, jnp.full((8, 128), off, I32), jnp.full((8, 128), cnt, I32))

    barrier = pltpu.get_barrier_semaphore()

    def greet(d):
        pl.semaphore_signal(barrier, inc=1, device_id=d, device_id_type=pl.DeviceIdType.MESH)

    for d in (z_up, z_dn, y_up, y_dn, sib):
        greet(d)

    @each
    def _(r, p):
        greet((p, j))

    pl.semaphore_wait(barrier, 5 + NDP - 1)

    def remote(src, dst, ssem, rsem, to):
        return pltpu.make_async_remote_copy(
            src_ref=src, dst_ref=dst, send_sem=ssem, recv_sem=rsem, device_id=to, device_id_type=pl.DeviceIdType.MESH
        )

    def rows(dz, par, start, size):
        zz = (z + dz + NZ) % NZ
        q = zz * 2 + (yl + par) % 2
        return wf.at[q, pl.ds(pl.multiple_of(256 * c + start, 16), size)]

    f0 = px * EXCL
    x0 = px * FETCH
    xo = (1 - px) * FETCH
    order = [(0, 0), (-1, 0), (1, 0), (0, 1), (-2, 0), (2, 0), (-1, 1), (1, 1),
             (-3, 0), (3, 0), (-2, 1), (2, 1), (4, 0), (-3, 1), (3, 1), (4, 1)]
    spot = {s: n for n, s in enumerate(order)}
    sends = []

    def send(src, ssem, rsem, to):
        copy = remote(src, src, ssem, rsem, to)
        copy.start()
        sends.append(copy)

    def arrived(ref, ssem, rsem):
        remote(ref, ref, ssem, rsem, sib).wait_recv()

    def chunk(dz, par, ch):
        return rows(dz, par, f0 + HALF * ch, HALF)

    def z_moves(hop, ch):
        return [(8 * d + 2 * (hop - 1) + ch, sign, to) for d, (sign, to) in enumerate(((-1, z_up), (1, z_dn)))
                if hop < 4 or d == ch]

    def send_z(hop, ch):
        for n, sign, to in z_moves(hop, ch):
            send(chunk(sign * (hop - 1), 0, ch), zs.at[n], zr.at[n], to)

    def wait_z(hop, ch):
        for n, sign, _ in z_moves(hop, ch):
            arrived(chunk(sign * hop if hop < 4 else 4, 0, ch), zs.at[n], zr.at[n])

    def send_y(dz, ch):
        n = 2 * (dz + 3) + ch
        send(chunk(dz, 0, ch), ys.at[n], yr.at[n], y_dn if ch else y_up)

    def wait_y(dz):
        for ch in range(2):
            n = 2 * (dz + 3) + ch
            arrived(chunk(dz, 1, ch), ys.at[n], yr.at[n])

    def send_x(dz, par):
        n = 2 * spot[dz, par]
        send(rows(dz, par, x0, XHALF), xs.at[n], xr.at[n], x_up)
        send(rows(dz, par, x0 + XHALF, XHALF), xs.at[n + 1], xr.at[n + 1], x_dn)

    def wait_x(dz, par):
        n = 2 * spot[dz, par]
        arrived(rows(dz, par, xo, XHALF), xs.at[n], xr.at[n])
        arrived(rows(dz, par, xo + XHALF, XHALF), xs.at[n + 1], xr.at[n + 1])

    def send_d(dz, par):
        n = spot[dz, par]
        send(rows(dz, par, 0, 256), ds_.at[n], dr.at[n], sib)

    def wait_d(dz, par):
        n = spot[dz, par]
        zz = (z + dz + NZ) % NZ
        q = zz * 2 + (yl + par) % 2
        ref = wf.at[q, pl.ds(pl.multiple_of(256 * (1 - c), 256), 256)]
        arrived(ref, ds_.at[n], dr.at[n])
        return q

    def both(step, k, *more):
        step(-k, *more)
        step(k, *more)

    def wait_x_send_d(dz, par):
        wait_x(dz, par)
        send_d(dz, par)

    def wait_y_send_x(dz):
        wait_y(dz)
        send_x(dz, 1)

    def hop_on(hop):
        for ch in range(2):
            wait_z(hop, ch)
            send_z(hop + 1, ch)
            both(send_y, hop, ch)
        both(send_x, hop, 0)

    own.wait()
    for ch in range(2):
        send_z(1, ch)
        send_y(0, ch)
    send_d(0, 0)

    @each
    def _(r, p):
        remote(meta.at[i], meta.at[i], ms.at[r], mr.at[r], (p, j)).start()

    acc[...] = jnp.zeros_like(acc)
    ups[...] = jnp.zeros_like(ups)
    local[2].wait()
    u = up_ref[...]
    high_part = u.astype(BF).astype(F32)
    ups[:, :, 0:32] = high_part
    ups[:, :, 32:64] = u - high_part

    hop_on(1)

    @each_from
    def _(r, p):
        remote(meta.at[p], meta.at[p], ms.at[r], mr.at[r], sib).wait_recv()

    def chosen(o, width, ref):
        o = jnp.broadcast_to(o[0:1, 0:1], (RANK, width))
        return jnp.where(o == 0, ref[0], jnp.where(o == 1, ref[1], ref[2]))

    def build(p, dst):
        o = meta[p]
        dst[:, 0:512] = chosen(o, 512, down_ref).astype(BF)
        dst[:, 512:640] = chosen(o, 128, ups).astype(BF)

    local[1].wait()

    @each
    def _(r, p):
        build(p, msg_out.at[p])
        remote(msg_out.at[p], msg_in.at[i], fs.at[r], fr.at[r], (p, j)).start()

    build(i, msg_in.at[i])

    def product(q):
        cols = pl.ds(pl.multiple_of(512 * q, 512), 512)
        acc[...] += dot(tok[:, cols], wf[q], PLAIN)

    wait_y_send_x(0)
    hop_on(2)
    both(wait_y_send_x, 1)
    both(wait_x_send_d, 1, 0)
    for copy in local[3:]:
        copy.wait()
    product(wait_d(0, 0))
    hop_on(3)
    both(wait_y_send_x, 2)
    wait_x_send_d(0, 1)
    both(wait_x_send_d, 2, 0)
    both(wait_x_send_d, 1, 1)
    for place in ((-1, 0), (1, 0), (0, 1)):
        product(wait_d(*place))
    for ch in range(2):
        wait_z(4, ch)
        send_y(4, ch)
    send_x(4, 0)
    both(wait_y_send_x, 3)
    both(wait_x_send_d, 3, 0)
    both(wait_x_send_d, 2, 1)
    for place in ((-2, 0), (2, 0), (-1, 1), (1, 1)):
        product(wait_d(*place))
    wait_y_send_x(4)
    wait_x_send_d(4, 0)
    both(wait_x_send_d, 3, 1)

    @each_from
    def _(r, p):
        remote(msg_in.at[p], msg_in.at[p], fs.at[r], fr.at[r], sib).wait_recv()

    def low(n, total):
        for k in range(4):
            p = 4 * n + k
            cols = pl.ds(pl.multiple_of(512 * p, 512), 512)
            total += dot(msg_in[p, :, 0:512], tok[:, cols], MINOR)
        return total

    lr_t = lax.fori_loop(0, NDP // 4, low, jnp.zeros((RANK, 128), F32))
    lane = lax.broadcasted_iota(I32, (RANK, 128), 1)
    for h in range(4):
        total = jnp.zeros((RANK, 128), F32)
        for q in range(4):
            t = msg_in[4 * h + q, :, 512:640].astype(F32)
            t = jnp.where(lane < 32, t + pltpu.roll(t, 96, 1), 0.0)
            total += pltpu.roll(t, 32 * q, 1) if q else t
        upf[:, 128 * h : 128 * h + 128] = total
    up_hi, up_lo = split(upf[...])
    lr_hi, lr_lo = split(lr_t)
    lr_hif, lr_lof = lr_hi.astype(F32), lr_lo.astype(F32)
    lr3 = jnp.concatenate([lr_hif, lr_lof, lr_hif], axis=0).T.astype(BF)
    extra = SCALE * dot(lr3, jnp.concatenate([up_hi, up_hi, up_lo], axis=0), PLAIN)
    for place in ((-3, 0), (3, 0), (-2, 1), (2, 1)):
        product(wait_d(*place))
    acc[...] += extra
    wait_x_send_d(4, 1)
    for place in ((4, 0), (-3, 1), (3, 1), (4, 1)):
        product(wait_d(*place))

    offs, cnts = meta[:, 0, :], meta[:, 4, :]
    total = jnp.sum(jnp.where(offs == off, cnts, 0), axis=0, keepdims=True).astype(F32)
    live = lax.broadcasted_iota(I32, (128, 128), 0) < cnt
    row_scale = jnp.where(live, jnp.broadcast_to(128.0 / total, (128, 128)), 0.0)
    gain = gain_ref[...]
    for h in range(4):
        cols = slice(128 * h, 128 * h + 128)
        projected = acc[:, cols]
        inverse = lax.rsqrt(jnp.mean(projected * projected, axis=-1, keepdims=True) + EPS)
        normed = projected * inverse
        keys_ref[:, cols] = (normed * gain).astype(BF)
        scaled = cot_ref[:, cols].astype(F32) * row_scale * gain
        along = jnp.mean(scaled * normed, axis=-1, keepdims=True)
        pg[:, cols] = inverse * (scaled - normed * along)
    pre_low, pre_rest = split(pg[...])

    def three(a_hi, a_lo, dims):
        parts = dot(jnp.concatenate([a_hi, a_lo], axis=0), pre_low, dims)
        return SCALE * (parts[0:RANK] + parts[RANK:] + dot(a_hi, pre_rest, dims))

    hi, lo = split(three(up_hi, up_lo, MINOR))
    lg_t2 = jnp.concatenate([hi, lo], axis=0)
    upf[...] = three(lr_hi, lr_lo, PLAIN)

    def grads(p, dst):
        cols = pl.ds(pl.multiple_of(512 * p, 512), 512)
        parts = dot(lg_t2, tok[:, cols], PLAIN)
        dst[:, 0:512] = (parts[0:RANK] + parts[RANK:]).astype(BF)
        v = pltpu.roll(upf[:, pl.ds(pl.multiple_of(128 * (p // 4), 128), 128)], (128 - 32 * (p % 4)) % 128, 1)
        rest = v - v.astype(BF).astype(F32)
        dst[:, 512:640] = jnp.where(lane < 32, v, jnp.where(lane < 64, pltpu.roll(rest, 32, 1), 0.0)).astype(BF)

    @each
    def _(r, p):
        grads(p, gmsg_out.at[p])
        remote(gmsg_out.at[p], gmsg_in.at[i], gs.at[r], gr.at[r], (p, j)).start()

    grads(i, gmsg_in.at[i])
    lg2 = jnp.concatenate([hi.astype(F32), lo.astype(F32)], axis=0).T.astype(BF)

    @pl.loop(0, NFS // 2)
    def _(q):
        cols = pl.ds(pl.multiple_of(512 * q, 512), 512)
        d = msg_in[q, :, 0:512]
        part = dot(lg2, jnp.concatenate([d, d], axis=0), PLAIN)
        ig[:, cols] = (part + dot(pre_low, wf[q], MINOR)).astype(BF)

    def gather(p, sums):
        o = jnp.broadcast_to(meta[p][0:1, 0:1], (RANK, 512))
        ou = o[:, 0:128]
        d = gmsg_in[p, :, 0:512].astype(F32)
        u = gmsg_in[p, :, 512:640].astype(F32)
        return tuple(
            (sd + jnp.where(o == s, d, 0.0), su + jnp.where(ou == s, u, 0.0)) for s, (sd, su) in enumerate(sums)
        )

    zero = (jnp.zeros((RANK, 512), F32), jnp.zeros((RANK, 128), F32))
    sums = gather(i, (zero,) * SLOTS)

    def later(r, p, sums):
        remote(gmsg_in.at[p], gmsg_in.at[p], gs.at[r], gr.at[r], sib).wait_recv()
        return gather(p, sums)

    for first, last in ORDER:
        sums = lax.fori_loop(first, last, lambda r, t: later(r, source(r), t), sums)
    for s, (sd, su) in enumerate(sums):
        down_out[s] = sd
        up_out[s] = (su + pltpu.roll(su, 96, 1))[:, 0:32]

    for copy in sends:
        copy.wait_send()

    @each
    def _(r, p):
        remote(meta.at[i], meta.at[i], ms.at[r], mr.at[r], (p, j)).wait_send()
        remote(msg_out.at[p], msg_in.at[i], fs.at[r], fr.at[r], (p, j)).wait_send()
        remote(gmsg_out.at[p], gmsg_in.at[i], gs.at[r], gr.at[r], (p, j)).wait_send()


def put_kernel(*refs):
    n = len(refs) // 2
    sem = refs[-1]
    copies = []
    for src, dst in zip(refs[:n], refs[n : 2 * n], strict=True):
        rows = src.shape[0]
        parts = 8 if rows == 128 and src.shape[1] > 1024 else 1
        for k in range(parts):
            cut = pl.ds(k * (rows // parts), rows // parts)
            copies.append(pltpu.make_async_copy(src.at[cut], dst.at[cut], sem.at[len(copies)]))
    for copy in copies:
        copy.start()
    for copy in copies:
        copy.wait()


def put(*arrays):
    hbm = pl.BlockSpec(memory_space=pltpu.MemorySpace.HBM)
    return pl.pallas_call(
        put_kernel,
        out_shape=tuple(jax.ShapeDtypeStruct(a.shape, a.dtype) for a in arrays),
        in_specs=[pl.BlockSpec(memory_space=pltpu.VMEM)] * len(arrays),
        out_specs=(hbm,) * len(arrays),
        scratch_shapes=[pltpu.SemaphoreType.DMA((16,))],
        name="put",
    )(*(pltpu.with_memory_space_constraint(a, pltpu.MemorySpace.VMEM) for a in arrays))


def stay(a):
    return pltpu.with_memory_space_constraint(a, pltpu.MemorySpace.HBM)


def on_device(tokens, weight, down, up, gain, offset, count, cot):
    n_rows, width = tokens.shape
    keys = cot.shape[1]
    vmem = pl.BlockSpec(memory_space=pltpu.VMEM)
    smem = pl.BlockSpec(memory_space=pltpu.SMEM)
    hbm = pl.BlockSpec(memory_space=pltpu.MemorySpace.HBM)
    dma = pltpu.SemaphoreType.DMA
    down_t = jnp.transpose(down, (0, 2, 1))
    out = pl.pallas_call(
        kernel,
        out_shape=(
            pltpu.VMEM((n_rows, keys), BF),
            pltpu.VMEM(down_t.shape, F32),
            pltpu.VMEM(up.shape, F32),
            pltpu.VMEM((n_rows, width), BF),
        ),
        in_specs=[smem] * 2 + [hbm] * 6,
        out_specs=(vmem,) * 4,
        scratch_shapes=[
            pltpu.VMEM((1, HD), F32),
            pltpu.VMEM(down_t.shape, F32),
            pltpu.VMEM(up.shape, F32),
            pltpu.VMEM((n_rows, keys), BF),
            pltpu.VMEM((NFS // 2, 512, keys), BF),
            pltpu.VMEM((n_rows, width), BF),
            pltpu.VMEM((n_rows, keys), F32),
            pltpu.VMEM((n_rows, keys), F32),
            pltpu.VMEM((NDP, 8, 128), I32),
            pltpu.VMEM((NDP, RANK, 640), BF),
            pltpu.VMEM((NDP, RANK, 640), BF),
            pltpu.VMEM((NDP, RANK, 640), BF),
            pltpu.VMEM((NDP, RANK, 640), BF),
            pltpu.VMEM((RANK, keys), F32),
            pltpu.VMEM((SLOTS, RANK, 128), F32),
            dma((8,)),
            dma((16,)), dma((16,)),
            dma((16,)), dma((16,)),
            dma((32,)), dma((32,)),
            dma((16,)), dma((16,)),
            dma((16,)), dma((16,)),
            dma((16,)), dma((16,)),
            dma((16,)), dma((16,)),
        ],
        compiler_params=pltpu.CompilerParams(
            collective_id=0, has_side_effects=True, vmem_limit_bytes=40 * 1024 * 1024
        ),
        name="key_projection",
    )(offset, count, *(stay(a) for a in (gain.reshape(1, HD), down_t, up, cot, tokens, weight)))
    keys_out, down_grad, up_grad, input_grad = put(*out)
    return keys_out, input_grad, jnp.transpose(down_grad, (0, 2, 1)), up_grad


def solution(mesh):
    rows = P(("dp", "fsdp"), None)
    down, up, cell = P("fsdp", "dp", None), P("fsdp", None, "dp"), P("dp", "fsdp")
    return jax.shard_map(
        on_device,
        mesh=mesh,
        in_specs=(rows, P("fsdp", None), down, up, P(), cell, cell, rows),
        out_specs=(rows, rows, down, up),
        check_vma=False,
    )
```

```python
import functools

import jax
import jax.numpy as jnp
from jax import lax
from jax.experimental import pallas as pl
from jax.experimental.pallas import tpu as pltpu
from jax.sharding import PartitionSpec as P

HD = 128
SCALE = 2.0
EPS = 1e-06
NX, NYH, NZ = 4, 4, 8
NDP = NX * NYH
NFS = NZ * 4
RANK = 16
SLOTS = 3
BF, F32, I32 = jnp.bfloat16, jnp.float32, jnp.int32
MINOR = (((1,), (1,)), ((), ()))
PLAIN = (((1,), (0,)), ((), ()))
EXCL = 96
FETCH = 256 - EXCL
HALF = FETCH // 2
XHALF = EXCL // 2


ORDER = ((8, 12), (4, 8), (12, 16), (1, 4))


def dot(a, b, dims, precision=None):
    return lax.dot_general(a, b, dims, precision=precision, preferred_element_type=F32)


def split(v):
    hi = v.astype(BF)
    return hi, (v - hi.astype(F32)).astype(BF)


def kernel(
    off_ref, cnt_ref, gain_hbm, down_hbm, up_hbm, cot_hbm, tok_hbm, w_hbm,
    keys_ref, down_out, up_out, ig,
    gain_ref, down_ref, up_ref, cot_ref, wf, tok, acc, pg, meta, msg_out, msg_in, gmsg_out, gmsg_in, upf, ups,
    loc_sem, zs, zr, ys, yr, xs, xr, ds_, dr, ms, mr, fs, fr, gs, gr,
):
    i, j = lax.axis_index("dp"), lax.axis_index("fsdp")
    yh, x = i // NX, i % NX
    z, yl, c = j // 4, (j // 2) % 2, j % 2
    px = x % 2

    def dp_of(a, b):
        return a * NX + b

    z_up = (i, (j + 4) % NFS)
    z_dn = (i, (j + NFS - 4) % NFS)
    sib = (i, j + 1 - 2 * c)
    jy = j + 2 - 4 * yl
    y_up = (dp_of((yh + yl) % NYH, x), jy)
    y_dn = (dp_of((yh + NYH - 1 + yl) % NYH, x), jy)
    x_up = (dp_of(yh, (x + 1) % NX), j)
    x_dn = (dp_of(yh, (x + NX - 1) % NX), j)

    def peer(r):
        return dp_of((yh + r // NX) % NYH, (x + r % NX) % NX)

    def source(r):
        return dp_of((yh + NYH - r // NX) % NYH, (x + NX - r % NX) % NX)

    def loops(who, unroll):
        def run(body):
            for first, last in ORDER:
                pl.loop(first, last, unroll=last - first if unroll else 1)(lambda r: body(r, who(r)))
        return run

    each, each_from, each_unrolled = loops(peer, False), loops(source, False), loops(peer, True)

    pair_me = j // 2
    local = [
        pltpu.make_async_copy(src, dst, loc_sem.at[n])
        for n, (src, dst) in enumerate((
            (w_hbm, wf.at[pair_me, pl.ds(pl.multiple_of(256 * c, 256), 256)]),
            (down_hbm, down_ref),
            (up_hbm, up_ref),
            (tok_hbm, tok),
            (gain_hbm, gain_ref),
            (cot_hbm, cot_ref),
        ))
    ]
    for copy in local:
        copy.start()
    own = local[0]
    off, cnt = off_ref[0, 0], cnt_ref[0, 0]
    rows8 = lax.broadcasted_iota(I32, (8, 128), 0)
    meta[i] = jnp.where(rows8 < 4, jnp.full((8, 128), off, I32), jnp.full((8, 128), cnt, I32))

    barrier = pltpu.get_barrier_semaphore()

    def greet(d):
        pl.semaphore_signal(barrier, inc=1, device_id=d, device_id_type=pl.DeviceIdType.MESH)

    for d in (z_up, z_dn, y_up, y_dn, sib):
        greet(d)

    @each
    def _(r, p):
        greet((p, j))

    pl.semaphore_wait(barrier, 5 + NDP - 1)

    def remote(src, dst, ssem, rsem, to):
        return pltpu.make_async_remote_copy(
            src_ref=src, dst_ref=dst, send_sem=ssem, recv_sem=rsem, device_id=to, device_id_type=pl.DeviceIdType.MESH
        )

    def rows(dz, par, start, size):
        zz = (z + dz + NZ) % NZ
        q = zz * 2 + (yl + par) % 2
        return wf.at[q, pl.ds(pl.multiple_of(256 * c + start, 16), size)]

    f0 = px * EXCL
    x0 = px * FETCH
    xo = (1 - px) * FETCH
    order = [(0, 0), (-1, 0), (1, 0), (0, 1), (-2, 0), (2, 0), (-1, 1), (1, 1),
             (-3, 0), (3, 0), (-2, 1), (2, 1), (4, 0), (-3, 1), (3, 1), (4, 1)]
    spot = {s: n for n, s in enumerate(order)}
    sends = []

    def send(src, ssem, rsem, to):
        copy = remote(src, src, ssem, rsem, to)
        copy.start()
        sends.append(copy)

    def arrived(ref, ssem, rsem):
        remote(ref, ref, ssem, rsem, sib).wait_recv()

    def chunk(dz, par, ch):
        return rows(dz, par, f0 + HALF * ch, HALF)

    def z_moves(hop, ch):
        return [(8 * d + 2 * (hop - 1) + ch, sign, to) for d, (sign, to) in enumerate(((-1, z_up), (1, z_dn)))
                if hop < 4 or d == ch]

    def send_z(hop, ch):
        for n, sign, to in z_moves(hop, ch):
            send(chunk(sign * (hop - 1), 0, ch), zs.at[n], zr.at[n], to)

    def wait_z(hop, ch):
        for n, sign, _ in z_moves(hop, ch):
            arrived(chunk(sign * hop if hop < 4 else 4, 0, ch), zs.at[n], zr.at[n])

    def send_y(dz, ch):
        n = 2 * (dz + 3) + ch
        send(chunk(dz, 0, ch), ys.at[n], yr.at[n], y_dn if ch else y_up)

    def wait_y(dz):
        for ch in range(2):
            n = 2 * (dz + 3) + ch
            arrived(chunk(dz, 1, ch), ys.at[n], yr.at[n])

    def send_x(dz, par):
        n = 2 * spot[dz, par]
        send(rows(dz, par, x0, XHALF), xs.at[n], xr.at[n], x_up)
        send(rows(dz, par, x0 + XHALF, XHALF), xs.at[n + 1], xr.at[n + 1], x_dn)

    def wait_x(dz, par):
        n = 2 * spot[dz, par]
        arrived(rows(dz, par, xo, XHALF), xs.at[n], xr.at[n])
        arrived(rows(dz, par, xo + XHALF, XHALF), xs.at[n + 1], xr.at[n + 1])

    def send_d(dz, par):
        n = spot[dz, par]
        send(rows(dz, par, 0, 256), ds_.at[n], dr.at[n], sib)

    def wait_d(dz, par):
        n = spot[dz, par]
        zz = (z + dz + NZ) % NZ
        q = zz * 2 + (yl + par) % 2
        ref = wf.at[q, pl.ds(pl.multiple_of(256 * (1 - c), 256), 256)]
        arrived(ref, ds_.at[n], dr.at[n])
        return q

    def both(step, k, *more):
        step(-k, *more)
        step(k, *more)

    def wait_x_send_d(dz, par):
        wait_x(dz, par)
        send_d(dz, par)

    def wait_y_send_x(dz):
        wait_y(dz)
        send_x(dz, 1)

    def hop_on(hop):
        for ch in range(2):
            wait_z(hop, ch)
            send_z(hop + 1, ch)
            if hop > 1:
                both(send_y, hop, ch)
        both(send_x, hop, 0)

    beside = ((7, -1, z_up), (14, 1, z_dn))

    own.wait()
    for ch in range(2):
        send_z(1, ch)
        send_y(0, ch)
    send_d(0, 0)

    @each
    def _(r, p):
        remote(meta.at[i], meta.at[i], ms.at[r], mr.at[r], (p, j)).start()

    acc[...] = jnp.zeros_like(acc)
    ups[...] = jnp.zeros_like(ups)
    local[2].wait()
    u = up_ref[...]
    high_part = u.astype(BF).astype(F32)
    ups[:, :, 0:32] = high_part
    ups[:, :, 32:64] = u - high_part

    hop_on(1)
    wait_y_send_x(0)
    for n, _, to in beside:
        send(rows(0, 1, f0, FETCH), zs.at[n], zr.at[n], to)

    @each_from
    def _(r, p):
        remote(meta.at[p], meta.at[p], ms.at[r], mr.at[r], sib).wait_recv()

    def chosen(o, width, ref):
        o = jnp.broadcast_to(o[0:1, 0:1], (RANK, width))
        return jnp.where(o == 0, ref[0], jnp.where(o == 1, ref[1], ref[2]))

    def build(p, dst):
        o = meta[p]
        dst[:, 0:512] = chosen(o, 512, down_ref).astype(BF)
        dst[:, 512:640] = chosen(o, 128, ups).astype(BF)

    local[1].wait()

    @each_unrolled
    def _(r, p):
        build(p, msg_out.at[p])
        remote(msg_out.at[p], msg_in.at[i], fs.at[r], fr.at[r], (p, j)).start()

    build(i, msg_in.at[i])

    def product(q):
        cols = pl.ds(pl.multiple_of(512 * q, 512), 512)
        acc[...] += dot(tok[:, cols], wf[q], PLAIN)

    hop_on(2)
    both(wait_x_send_d, 1, 0)
    for copy in local[3:]:
        copy.wait()
    product(wait_d(0, 0))
    hop_on(3)
    for n, sign, _ in beside:
        arrived(rows(sign, 1, f0, FETCH), zs.at[n], zr.at[n])
        send_x(sign, 1)
    both(wait_y_send_x, 2)
    wait_x_send_d(0, 1)
    both(wait_x_send_d, 2, 0)
    for place in ((-1, 0), (1, 0), (0, 1)):
        product(wait_d(*place))
    for ch in range(2):
        wait_z(4, ch)
        send_y(4, ch)
    send_x(4, 0)
    both(wait_y_send_x, 3)
    both(wait_x_send_d, 1, 1)
    both(wait_x_send_d, 3, 0)
    both(wait_x_send_d, 2, 1)
    for place in ((-2, 0), (2, 0), (-1, 1), (1, 1)):
        product(wait_d(*place))
    wait_y_send_x(4)
    wait_x_send_d(4, 0)
    both(wait_x_send_d, 3, 1)

    @each_from
    def _(r, p):
        remote(msg_in.at[p], msg_in.at[p], fs.at[r], fr.at[r], sib).wait_recv()

    def low(n, total):
        for k in range(4):
            p = 4 * n + k
            cols = pl.ds(pl.multiple_of(512 * p, 512), 512)
            total += dot(msg_in[p, :, 0:512], tok[:, cols], MINOR)
        return total

    lr_t = lax.fori_loop(0, NDP // 4, low, jnp.zeros((RANK, 128), F32))
    lane = lax.broadcasted_iota(I32, (RANK, 128), 1)
    for h in range(4):
        total = jnp.zeros((RANK, 128), F32)
        for q in range(4):
            t = msg_in[4 * h + q, :, 512:640].astype(F32)
            t = jnp.where(lane < 32, t + pltpu.roll(t, 96, 1), 0.0)
            total += pltpu.roll(t, 32 * q, 1) if q else t
        upf[:, 128 * h : 128 * h + 128] = total
    up_hi, up_lo = split(upf[...])
    lr_hi, lr_lo = split(lr_t)
    lr_hif, lr_lof = lr_hi.astype(F32), lr_lo.astype(F32)
    lr3 = jnp.concatenate([lr_hif, lr_lof, lr_hif], axis=0).T.astype(BF)
    extra = SCALE * dot(lr3, jnp.concatenate([up_hi, up_hi, up_lo], axis=0), PLAIN)
    for place in ((-3, 0), (3, 0), (-2, 1), (2, 1)):
        product(wait_d(*place))
    acc[...] += extra
    wait_x_send_d(4, 1)
    for place in ((4, 0), (-3, 1), (3, 1), (4, 1)):
        product(wait_d(*place))

    offs, cnts = meta[:, 0, :], meta[:, 4, :]
    total = jnp.sum(jnp.where(offs == off, cnts, 0), axis=0, keepdims=True).astype(F32)
    live = lax.broadcasted_iota(I32, (128, 128), 0) < cnt
    row_scale = jnp.where(live, jnp.broadcast_to(128.0 / total, (128, 128)), 0.0)
    gain = gain_ref[...]
    for h in range(4):
        cols = slice(128 * h, 128 * h + 128)
        projected = acc[:, cols]
        inverse = lax.rsqrt(jnp.mean(projected * projected, axis=-1, keepdims=True) + EPS)
        normed = projected * inverse
        keys_ref[:, cols] = (normed * gain).astype(BF)
        scaled = cot_ref[:, cols].astype(F32) * row_scale * gain
        along = jnp.mean(scaled * normed, axis=-1, keepdims=True)
        pg[:, cols] = inverse * (scaled - normed * along)
    pre_low, pre_rest = split(pg[...])

    def three(a_hi, a_lo, dims):
        parts = dot(jnp.concatenate([a_hi, a_lo], axis=0), pre_low, dims)
        return SCALE * (parts[0:RANK] + parts[RANK:] + dot(a_hi, pre_rest, dims))

    hi, lo = split(three(up_hi, up_lo, MINOR))
    lg_t2 = jnp.concatenate([hi, lo], axis=0)
    upf[...] = three(lr_hi, lr_lo, PLAIN)

    def grads(p, dst):
        cols = pl.ds(pl.multiple_of(512 * p, 512), 512)
        parts = dot(lg_t2, tok[:, cols], PLAIN)
        dst[:, 0:512] = (parts[0:RANK] + parts[RANK:]).astype(BF)
        v = pltpu.roll(upf[:, pl.ds(pl.multiple_of(128 * (p // 4), 128), 128)], (128 - 32 * (p % 4)) % 128, 1)
        rest = v - v.astype(BF).astype(F32)
        dst[:, 512:640] = jnp.where(lane < 32, v, jnp.where(lane < 64, pltpu.roll(rest, 32, 1), 0.0)).astype(BF)

    @each_unrolled
    def _(r, p):
        grads(p, gmsg_out.at[p])
        remote(gmsg_out.at[p], gmsg_in.at[i], gs.at[r], gr.at[r], (p, j)).start()

    grads(i, gmsg_in.at[i])
    lg2 = jnp.concatenate([hi.astype(F32), lo.astype(F32)], axis=0).T.astype(BF)

    @pl.loop(0, NFS // 2, unroll=4)
    def _(q):
        cols = pl.ds(pl.multiple_of(512 * q, 512), 512)
        d = msg_in[q, :, 0:512]
        part = dot(lg2, jnp.concatenate([d, d], axis=0), PLAIN)
        ig[:, cols] = (part + dot(pre_low, wf[q], MINOR)).astype(BF)

    def gather(p, sums):
        o = jnp.broadcast_to(meta[p][0:1, 0:1], (RANK, 512))
        ou = o[:, 0:128]
        d = gmsg_in[p, :, 0:512].astype(F32)
        u = gmsg_in[p, :, 512:640].astype(F32)
        return tuple(
            (sd + jnp.where(o == s, d, 0.0), su + jnp.where(ou == s, u, 0.0)) for s, (sd, su) in enumerate(sums)
        )

    zero = (jnp.zeros((RANK, 512), F32), jnp.zeros((RANK, 128), F32))
    sums = gather(i, (zero,) * SLOTS)

    def later(r, p, sums):
        remote(gmsg_in.at[p], gmsg_in.at[p], gs.at[r], gr.at[r], sib).wait_recv()
        return gather(p, sums)

    for first, last in ORDER:
        sums = lax.fori_loop(first, last, lambda r, t: later(r, source(r), t), sums, unroll=True)
    for s, (sd, su) in enumerate(sums):
        down_out[s] = sd
        up_out[s] = (su + pltpu.roll(su, 96, 1))[:, 0:32]

    for copy in sends:
        copy.wait_send()

    @each
    def _(r, p):
        remote(meta.at[i], meta.at[i], ms.at[r], mr.at[r], (p, j)).wait_send()
        remote(msg_out.at[p], msg_in.at[i], fs.at[r], fr.at[r], (p, j)).wait_send()
        remote(gmsg_out.at[p], gmsg_in.at[i], gs.at[r], gr.at[r], (p, j)).wait_send()


def put_kernel(*refs):
    n = len(refs) // 2
    sem = refs[-1]
    copies = []
    for src, dst in zip(refs[:n], refs[n : 2 * n], strict=True):
        rows = src.shape[0]
        parts = 8 if rows == 128 and src.shape[1] > 1024 else 1
        for k in range(parts):
            cut = pl.ds(k * (rows // parts), rows // parts)
            copies.append(pltpu.make_async_copy(src.at[cut], dst.at[cut], sem.at[len(copies)]))
    for copy in copies:
        copy.start()
    for copy in copies:
        copy.wait()


def put(*arrays):
    hbm = pl.BlockSpec(memory_space=pltpu.MemorySpace.HBM)
    return pl.pallas_call(
        put_kernel,
        out_shape=tuple(jax.ShapeDtypeStruct(a.shape, a.dtype) for a in arrays),
        in_specs=[pl.BlockSpec(memory_space=pltpu.VMEM)] * len(arrays),
        out_specs=(hbm,) * len(arrays),
        scratch_shapes=[pltpu.SemaphoreType.DMA((16,))],
        name="put",
    )(*(pltpu.with_memory_space_constraint(a, pltpu.MemorySpace.VMEM) for a in arrays))


def stay(a):
    return pltpu.with_memory_space_constraint(a, pltpu.MemorySpace.HBM)


def on_device(tokens, weight, down, up, gain, offset, count, cot):
    n_rows, width = tokens.shape
    keys = cot.shape[1]
    vmem = pl.BlockSpec(memory_space=pltpu.VMEM)
    smem = pl.BlockSpec(memory_space=pltpu.SMEM)
    hbm = pl.BlockSpec(memory_space=pltpu.MemorySpace.HBM)
    dma = pltpu.SemaphoreType.DMA
    down_t = jnp.transpose(down, (0, 2, 1))
    out = pl.pallas_call(
        kernel,
        out_shape=(
            pltpu.VMEM((n_rows, keys), BF),
            pltpu.VMEM(down_t.shape, F32),
            pltpu.VMEM(up.shape, F32),
            pltpu.VMEM((n_rows, width), BF),
        ),
        in_specs=[smem] * 2 + [hbm] * 6,
        out_specs=(vmem,) * 4,
        scratch_shapes=[
            pltpu.VMEM((1, HD), F32),
            pltpu.VMEM(down_t.shape, F32),
            pltpu.VMEM(up.shape, F32),
            pltpu.VMEM((n_rows, keys), BF),
            pltpu.VMEM((NFS // 2, 512, keys), BF),
            pltpu.VMEM((n_rows, width), BF),
            pltpu.VMEM((n_rows, keys), F32),
            pltpu.VMEM((n_rows, keys), F32),
            pltpu.VMEM((NDP, 8, 128), I32),
            pltpu.VMEM((NDP, RANK, 640), BF),
            pltpu.VMEM((NDP, RANK, 640), BF),
            pltpu.VMEM((NDP, RANK, 640), BF),
            pltpu.VMEM((NDP, RANK, 640), BF),
            pltpu.VMEM((RANK, keys), F32),
            pltpu.VMEM((SLOTS, RANK, 128), F32),
            dma((8,)),
            dma((16,)), dma((16,)),
            dma((16,)), dma((16,)),
            dma((32,)), dma((32,)),
            dma((16,)), dma((16,)),
            dma((16,)), dma((16,)),
            dma((16,)), dma((16,)),
            dma((16,)), dma((16,)),
        ],
        compiler_params=pltpu.CompilerParams(
            collective_id=0, has_side_effects=True, vmem_limit_bytes=40 * 1024 * 1024
        ),
        name="key_projection",
    )(offset, count, *(stay(a) for a in (gain.reshape(1, HD), down_t, up, cot, tokens, weight)))
    keys_out, down_grad, up_grad, input_grad = put(*out)
    return keys_out, input_grad, jnp.transpose(down_grad, (0, 2, 1)), up_grad


def solution(mesh):
    rows = P(("dp", "fsdp"), None)
    down, up, cell = P("fsdp", "dp", None), P("fsdp", None, "dp"), P("dp", "fsdp")
    return jax.shard_map(
        on_device,
        mesh=mesh,
        in_specs=(rows, P("fsdp", None), down, up, P(), cell, cell, rows),
        out_specs=(rows, rows, down, up),
        check_vma=False,
    )
```

```python
import functools

import jax
import jax.numpy as jnp
from jax import lax
from jax.experimental import pallas as pl
from jax.experimental.pallas import tpu as pltpu
from jax.sharding import PartitionSpec as P

HD = 128
SCALE = 2.0
EPS = 1e-06
NX, NYH, NZ = 4, 4, 8
NDP = NX * NYH
NFS = NZ * 4
RANK = 16
SLOTS = 3
BF, F32, I32 = jnp.bfloat16, jnp.float32, jnp.int32
MINOR = (((1,), (1,)), ((), ()))
PLAIN = (((1,), (0,)), ((), ()))
EXCL = 96
FETCH = 256 - EXCL
HALF = FETCH // 2
XHALF = EXCL // 2


ORDER = ((8, 12), (4, 8), (12, 16), (1, 4))


def dot(a, b, dims, precision=None):
    return lax.dot_general(a, b, dims, precision=precision, preferred_element_type=F32)


def split(v):
    hi = v.astype(BF)
    return hi, (v - hi.astype(F32)).astype(BF)


def kernel(
    off_ref, cnt_ref, gain_hbm, down_hbm, up_hbm, cot_hbm, tok_hbm, w_hbm,
    keys_ref, down_out, up_out, ig,
    gain_ref, down_ref, up_ref, cot_ref, wf, tok, acc, pg, meta, msg_out, msg_in, gmsg_out, gmsg_in, upf, ups,
    loc_sem, zs, zr, ys, yr, xs, xr, ds_, dr, ms, mr, fs, fr, gs, gr,
):
    i, j = lax.axis_index("dp"), lax.axis_index("fsdp")
    yh, x = i // NX, i % NX
    z, yl, c = j // 4, (j // 2) % 2, j % 2
    px = x % 2

    def dp_of(a, b):
        return a * NX + b

    z_up = (i, (j + 4) % NFS)
    z_dn = (i, (j + NFS - 4) % NFS)
    sib = (i, j + 1 - 2 * c)
    jy = j + 2 - 4 * yl
    y_up = (dp_of((yh + yl) % NYH, x), jy)
    y_dn = (dp_of((yh + NYH - 1 + yl) % NYH, x), jy)
    x_up = (dp_of(yh, (x + 1) % NX), j)
    x_dn = (dp_of(yh, (x + NX - 1) % NX), j)

    def peer(r):
        return dp_of((yh + r // NX) % NYH, (x + r % NX) % NX)

    def source(r):
        return dp_of((yh + NYH - r // NX) % NYH, (x + NX - r % NX) % NX)

    def loops(who, unroll):
        def run(body):
            for first, last in ORDER:
                pl.loop(first, last, unroll=last - first if unroll else 1)(lambda r: body(r, who(r)))
        return run

    each, each_from, each_unrolled = loops(peer, False), loops(source, False), loops(peer, True)

    pair_me = j // 2
    local = [
        pltpu.make_async_copy(src, dst, loc_sem.at[n])
        for n, (src, dst) in enumerate((
            (w_hbm, wf.at[pair_me, pl.ds(pl.multiple_of(256 * c, 256), 256)]),
            (down_hbm, down_ref),
            (up_hbm, up_ref),
            (tok_hbm, tok),
            (gain_hbm, gain_ref),
            (cot_hbm, cot_ref),
        ))
    ]
    for copy in local:
        copy.start()
    own = local[0]
    off, cnt = off_ref[0, 0], cnt_ref[0, 0]
    rows8 = lax.broadcasted_iota(I32, (8, 128), 0)
    meta[i] = jnp.where(rows8 < 4, jnp.full((8, 128), off, I32), jnp.full((8, 128), cnt, I32))

    barrier = pltpu.get_barrier_semaphore()

    def greet(d):
        pl.semaphore_signal(barrier, inc=1, device_id=d, device_id_type=pl.DeviceIdType.MESH)

    for d in (z_up, z_dn, y_up, y_dn, sib):
        greet(d)

    @each
    def _(r, p):
        greet((p, j))

    pl.semaphore_wait(barrier, 5 + NDP - 1)

    def remote(src, dst, ssem, rsem, to):
        return pltpu.make_async_remote_copy(
            src_ref=src, dst_ref=dst, send_sem=ssem, recv_sem=rsem, device_id=to, device_id_type=pl.DeviceIdType.MESH
        )

    def rows(dz, par, start, size):
        zz = (z + dz + NZ) % NZ
        q = zz * 2 + (yl + par) % 2
        return wf.at[q, pl.ds(pl.multiple_of(256 * c + start, 16), size)]

    f0 = px * EXCL
    x0 = px * FETCH
    xo = (1 - px) * FETCH
    order = [(0, 0), (-1, 0), (1, 0), (0, 1), (-2, 0), (2, 0), (-1, 1), (1, 1),
             (-3, 0), (3, 0), (-2, 1), (2, 1), (4, 0), (-3, 1), (3, 1), (4, 1)]
    spot = {s: n for n, s in enumerate(order)}
    sends = []

    def send(src, ssem, rsem, to):
        copy = remote(src, src, ssem, rsem, to)
        copy.start()
        sends.append(copy)

    def arrived(ref, ssem, rsem):
        remote(ref, ref, ssem, rsem, sib).wait_recv()

    def chunk(dz, par, ch):
        return rows(dz, par, f0 + HALF * ch, HALF)

    def z_moves(hop, ch):
        return [(8 * d + 2 * (hop - 1) + ch, sign, to) for d, (sign, to) in enumerate(((-1, z_up), (1, z_dn)))
                if hop < 4 or d == ch]

    def send_z(hop, ch):
        for n, sign, to in z_moves(hop, ch):
            send(chunk(sign * (hop - 1), 0, ch), zs.at[n], zr.at[n], to)

    def wait_z(hop, ch):
        for n, sign, _ in z_moves(hop, ch):
            arrived(chunk(sign * hop if hop < 4 else 4, 0, ch), zs.at[n], zr.at[n])

    def send_y(dz, ch):
        n = 2 * (dz + 3) + ch
        send(chunk(dz, 0, ch), ys.at[n], yr.at[n], y_dn if ch else y_up)

    def wait_y(dz):
        for ch in range(2):
            n = 2 * (dz + 3) + ch
            arrived(chunk(dz, 1, ch), ys.at[n], yr.at[n])

    def send_x(dz, par):
        n = 2 * spot[dz, par]
        send(rows(dz, par, x0, XHALF), xs.at[n], xr.at[n], x_up)
        send(rows(dz, par, x0 + XHALF, XHALF), xs.at[n + 1], xr.at[n + 1], x_dn)

    def wait_x(dz, par):
        n = 2 * spot[dz, par]
        arrived(rows(dz, par, xo, XHALF), xs.at[n], xr.at[n])
        arrived(rows(dz, par, xo + XHALF, XHALF), xs.at[n + 1], xr.at[n + 1])

    def send_d(dz, par):
        n = spot[dz, par]
        send(rows(dz, par, 0, 256), ds_.at[n], dr.at[n], sib)

    def wait_d(dz, par):
        n = spot[dz, par]
        zz = (z + dz + NZ) % NZ
        q = zz * 2 + (yl + par) % 2
        ref = wf.at[q, pl.ds(pl.multiple_of(256 * (1 - c), 256), 256)]
        arrived(ref, ds_.at[n], dr.at[n])
        return q

    def both(step, k, *more):
        step(-k, *more)
        step(k, *more)

    def wait_x_send_d(dz, par):
        wait_x(dz, par)
        send_d(dz, par)

    def wait_y_send_x(dz):
        wait_y(dz)
        send_x(dz, 1)

    def hop_on(hop):
        for ch in range(2):
            wait_z(hop, ch)
            send_z(hop + 1, ch)
            if hop > 1:
                both(send_y, hop, ch)
        both(send_x, hop, 0)

    beside = ((7, -1, z_up), (14, 1, z_dn))

    own.wait()
    for ch in range(2):
        send_z(1, ch)
        send_y(0, ch)
    send_d(0, 0)

    @each
    def _(r, p):
        remote(meta.at[i], meta.at[i], ms.at[r], mr.at[r], (p, j)).start()

    acc[...] = jnp.zeros_like(acc)
    ups[...] = jnp.zeros_like(ups)
    local[2].wait()
    u = up_ref[...]
    high_part = u.astype(BF).astype(F32)
    ups[:, :, 0:32] = high_part
    ups[:, :, 32:64] = u - high_part

    hop_on(1)
    wait_y_send_x(0)
    for n, _, to in beside:
        send(rows(0, 1, f0, FETCH), zs.at[n], zr.at[n], to)

    @each_from
    def _(r, p):
        remote(meta.at[p], meta.at[p], ms.at[r], mr.at[r], sib).wait_recv()

    def chosen(o, width, ref):
        o = jnp.broadcast_to(o[0:1, 0:1], (RANK, width))
        return jnp.where(o == 0, ref[0], jnp.where(o == 1, ref[1], ref[2]))

    def build(p, dst):
        o = meta[p]
        dst[:, 0:512] = chosen(o, 512, down_ref).astype(BF)
        dst[:, 512:640] = chosen(o, 128, ups).astype(BF)

    local[1].wait()

    @each_unrolled
    def _(r, p):
        build(p, msg_out.at[p])
        remote(msg_out.at[p], msg_in.at[i], fs.at[r], fr.at[r], (p, j)).start()

    build(i, msg_in.at[i])

    def products(*places):
        total = acc[...]
        for place in places:
            q = wait_d(*place)
            total += dot(tok[:, pl.ds(pl.multiple_of(512 * q, 512), 512)], wf[q], PLAIN)
        acc[...] = total

    hop_on(2)
    both(wait_x_send_d, 1, 0)
    for copy in local[3:]:
        copy.wait()
    products((0, 0))
    hop_on(3)
    for n, sign, _ in beside:
        arrived(rows(sign, 1, f0, FETCH), zs.at[n], zr.at[n])
        send_x(sign, 1)
    both(wait_y_send_x, 2)
    wait_x_send_d(0, 1)
    both(wait_x_send_d, 2, 0)
    products((-1, 0), (1, 0), (0, 1))
    def low_of(p):
        cols = pl.ds(pl.multiple_of(512 * p, 512), 512)
        return dot(msg_in[p, :, 0:512], tok[:, cols], MINOR)

    def low(group, total):
        @pl.loop(*group)
        def _(r):
            p = source(r)
            remote(msg_in.at[p], msg_in.at[p], fs.at[r], fr.at[r], sib).wait_recv()

        for r in range(*group):
            total += low_of(source(r))
        return total

    lr_t = low_of(i)
    for ch in range(2):
        wait_z(4, ch)
        send_y(4, ch)
    send_x(4, 0)
    both(wait_y_send_x, 3)
    both(wait_x_send_d, 1, 1)
    both(wait_x_send_d, 3, 0)
    both(wait_x_send_d, 2, 1)
    products((-2, 0), (2, 0), (-1, 1), (1, 1))
    wait_y_send_x(4)
    wait_x_send_d(4, 0)
    both(wait_x_send_d, 3, 1)

    offs, cnts = meta[:, 0, :], meta[:, 4, :]
    total = jnp.sum(jnp.where(offs == off, cnts, 0), axis=0, keepdims=True).astype(F32)
    live = lax.broadcasted_iota(I32, (128, 128), 0) < cnt
    row_scale = jnp.where(live, jnp.broadcast_to(128.0 / total, (128, 128)), 0.0)
    gain = gain_ref[...]
    for h in range(4):
        cols = slice(128 * h, 128 * h + 128)
        pg[:, cols] = cot_ref[:, cols].astype(F32) * row_scale * gain

    for group in ((1, 4), (12, 16), (4, 8), (8, 12)):
        lr_t = low(group, lr_t)
    lane = lax.broadcasted_iota(I32, (RANK, 128), 1)
    for h in range(4):
        total = jnp.zeros((RANK, 128), F32)
        for q in range(4):
            t = msg_in[4 * h + q, :, 512:640].astype(F32)
            t = jnp.where(lane < 32, t + pltpu.roll(t, 96, 1), 0.0)
            total += pltpu.roll(t, 32 * q, 1) if q else t
        upf[:, 128 * h : 128 * h + 128] = total
    up_hi, up_lo = split(upf[...])
    lr_hi, lr_lo = split(lr_t)
    lr_hif, lr_lof = lr_hi.astype(F32), lr_lo.astype(F32)
    lr3 = jnp.concatenate([lr_hif, lr_lof, lr_hif], axis=0).T.astype(BF)
    extra = SCALE * dot(lr3, jnp.concatenate([up_hi, up_hi, up_lo], axis=0), PLAIN)
    products((-3, 0), (3, 0), (-2, 1), (2, 1))
    acc[...] += extra
    wait_x_send_d(4, 1)
    products((4, 0), (-3, 1), (3, 1), (4, 1))

    for h in range(4):
        cols = slice(128 * h, 128 * h + 128)
        projected = acc[:, cols]
        inverse = lax.rsqrt(jnp.mean(projected * projected, axis=-1, keepdims=True) + EPS)
        normed = projected * inverse
        keys_ref[:, cols] = (normed * gain).astype(BF)
        scaled = pg[:, cols]
        along = jnp.mean(scaled * normed, axis=-1, keepdims=True)
        pg[:, cols] = inverse * (scaled - normed * along)
    pre_low, pre_rest = split(pg[...])

    def three(a_hi, a_lo, dims):
        parts = dot(jnp.concatenate([a_hi, a_lo], axis=0), pre_low, dims)
        return SCALE * (parts[0:RANK] + parts[RANK:] + dot(a_hi, pre_rest, dims))

    hi, lo = split(three(up_hi, up_lo, MINOR))
    lg_t2 = jnp.concatenate([hi, lo], axis=0)
    upf[...] = three(lr_hi, lr_lo, PLAIN)

    def grads(p, dst):
        cols = pl.ds(pl.multiple_of(512 * p, 512), 512)
        parts = dot(lg_t2, tok[:, cols], PLAIN)
        dst[:, 0:512] = (parts[0:RANK] + parts[RANK:]).astype(BF)
        v = pltpu.roll(upf[:, pl.ds(pl.multiple_of(128 * (p // 4), 128), 128)], (128 - 32 * (p % 4)) % 128, 1)
        rest = v - v.astype(BF).astype(F32)
        dst[:, 512:640] = jnp.where(lane < 32, v, jnp.where(lane < 64, pltpu.roll(rest, 32, 1), 0.0)).astype(BF)

    @each_unrolled
    def _(r, p):
        grads(p, gmsg_out.at[p])
        remote(gmsg_out.at[p], gmsg_in.at[i], gs.at[r], gr.at[r], (p, j)).start()

    grads(i, gmsg_in.at[i])
    lg2 = jnp.concatenate([hi.astype(F32), lo.astype(F32)], axis=0).T.astype(BF)

    @pl.loop(0, NFS // 2, unroll=4)
    def _(q):
        cols = pl.ds(pl.multiple_of(512 * q, 512), 512)
        d = msg_in[q, :, 0:512]
        part = dot(lg2, jnp.concatenate([d, d], axis=0), PLAIN)
        ig[:, cols] = (part + dot(pre_low, wf[q], MINOR)).astype(BF)

    def gather(p, sums):
        o = jnp.broadcast_to(meta[p][0:1, 0:1], (RANK, 512))
        ou = o[:, 0:128]
        d = gmsg_in[p, :, 0:512].astype(F32)
        u = gmsg_in[p, :, 512:640].astype(F32)
        return tuple(
            (sd + jnp.where(o == s, d, 0.0), su + jnp.where(ou == s, u, 0.0)) for s, (sd, su) in enumerate(sums)
        )

    zero = (jnp.zeros((RANK, 512), F32), jnp.zeros((RANK, 128), F32))
    sums = gather(i, (zero,) * SLOTS)

    def later(r, p, sums):
        remote(gmsg_in.at[p], gmsg_in.at[p], gs.at[r], gr.at[r], sib).wait_recv()
        return gather(p, sums)

    for first, last in ORDER:
        sums = lax.fori_loop(first, last, lambda r, t: later(r, source(r), t), sums, unroll=True)
    for s, (sd, su) in enumerate(sums):
        down_out[s] = sd
        up_out[s] = (su + pltpu.roll(su, 96, 1))[:, 0:32]

    for copy in sends:
        copy.wait_send()

    @each
    def _(r, p):
        remote(meta.at[i], meta.at[i], ms.at[r], mr.at[r], (p, j)).wait_send()
        remote(msg_out.at[p], msg_in.at[i], fs.at[r], fr.at[r], (p, j)).wait_send()
        remote(gmsg_out.at[p], gmsg_in.at[i], gs.at[r], gr.at[r], (p, j)).wait_send()


def put_kernel(*refs):
    n = len(refs) // 2
    sem = refs[-1]
    copies = []
    for src, dst in zip(refs[:n], refs[n : 2 * n], strict=True):
        rows = src.shape[0]
        parts = 8 if rows == 128 and src.shape[1] > 1024 else 1
        for k in range(parts):
            cut = pl.ds(k * (rows // parts), rows // parts)
            copies.append(pltpu.make_async_copy(src.at[cut], dst.at[cut], sem.at[len(copies)]))
    for copy in copies:
        copy.start()
    for copy in copies:
        copy.wait()


def put(*arrays):
    hbm = pl.BlockSpec(memory_space=pltpu.MemorySpace.HBM)
    return pl.pallas_call(
        put_kernel,
        out_shape=tuple(jax.ShapeDtypeStruct(a.shape, a.dtype) for a in arrays),
        in_specs=[pl.BlockSpec(memory_space=pltpu.VMEM)] * len(arrays),
        out_specs=(hbm,) * len(arrays),
        scratch_shapes=[pltpu.SemaphoreType.DMA((16,))],
        name="put",
    )(*(pltpu.with_memory_space_constraint(a, pltpu.MemorySpace.VMEM) for a in arrays))


def stay(a):
    return pltpu.with_memory_space_constraint(a, pltpu.MemorySpace.HBM)


def on_device(tokens, weight, down, up, gain, offset, count, cot):
    n_rows, width = tokens.shape
    keys = cot.shape[1]
    vmem = pl.BlockSpec(memory_space=pltpu.VMEM)
    smem = pl.BlockSpec(memory_space=pltpu.SMEM)
    hbm = pl.BlockSpec(memory_space=pltpu.MemorySpace.HBM)
    dma = pltpu.SemaphoreType.DMA
    down_t = jnp.transpose(down, (0, 2, 1))
    out = pl.pallas_call(
        kernel,
        out_shape=(
            pltpu.VMEM((n_rows, keys), BF),
            pltpu.VMEM(down_t.shape, F32),
            pltpu.VMEM(up.shape, F32),
            pltpu.VMEM((n_rows, width), BF),
        ),
        in_specs=[smem] * 2 + [hbm] * 6,
        out_specs=(vmem,) * 4,
        scratch_shapes=[
            pltpu.VMEM((1, HD), F32),
            pltpu.VMEM(down_t.shape, F32),
            pltpu.VMEM(up.shape, F32),
            pltpu.VMEM((n_rows, keys), BF),
            pltpu.VMEM((NFS // 2, 512, keys), BF),
            pltpu.VMEM((n_rows, width), BF),
            pltpu.VMEM((n_rows, keys), F32),
            pltpu.VMEM((n_rows, keys), F32),
            pltpu.VMEM((NDP, 8, 128), I32),
            pltpu.VMEM((NDP, RANK, 640), BF),
            pltpu.VMEM((NDP, RANK, 640), BF),
            pltpu.VMEM((NDP, RANK, 640), BF),
            pltpu.VMEM((NDP, RANK, 640), BF),
            pltpu.VMEM((RANK, keys), F32),
            pltpu.VMEM((SLOTS, RANK, 128), F32),
            dma((8,)),
            dma((16,)), dma((16,)),
            dma((16,)), dma((16,)),
            dma((32,)), dma((32,)),
            dma((16,)), dma((16,)),
            dma((16,)), dma((16,)),
            dma((16,)), dma((16,)),
            dma((16,)), dma((16,)),
        ],
        compiler_params=pltpu.CompilerParams(
            collective_id=0, has_side_effects=True, vmem_limit_bytes=40 * 1024 * 1024
        ),
        name="key_projection",
    )(offset, count, *(stay(a) for a in (gain.reshape(1, HD), down_t, up, cot, tokens, weight)))
    keys_out, down_grad, up_grad, input_grad = put(*out)
    return keys_out, input_grad, jnp.transpose(down_grad, (0, 2, 1)), up_grad


def solution(mesh):
    rows = P(("dp", "fsdp"), None)
    down, up, cell = P("fsdp", "dp", None), P("fsdp", None, "dp"), P("dp", "fsdp")
    return jax.shard_map(
        on_device,
        mesh=mesh,
        in_specs=(rows, P("fsdp", None), down, up, P(), cell, cell, rows),
        out_specs=(rows, rows, down, up),
        check_vma=False,
    )
```
